256 devices in a mesh: ctx: 64 (over x, z, core), tp: 4 (over y).
Axes of the slice: x: 4, y: 4, z: 8, core: 2. Of those that a mesh axis runs over, the one named last changes fastest.
Arguments:
- tokens: bfloat16 [8192, 4096], P('ctx', 'tp'), may hold values from -70 to 70
- norm_gain: float32 [4096], P('tp'), may hold values from 0.5 to 1.5
- short_filter: float32 [3, 3, 4096], P(None, None, 'tp'), may hold values from -3.6 to 3.6
- medium_filter: float32 [128, 4096], P(None, 'tp'), may hold values from -0.5 to 0.5
- residues: float32 [4096, 16], P(('tp', 'ctx')), may hold values from -2.1 to 2.1
- decay_rate: float32 [4096, 16], P(('tp', 'ctx')), may hold values from 0.5 to 500
- skip_gain: float32 [4096], P(('tp', 'ctx')), may hold values from -4 to 4
- grad_out: bfloat16 [8192, 4096], P('ctx', 'tp'), may hold values from -6 to 6
Outputs:
- block_out: bfloat16 [8192, 4096], P('ctx', 'tp')
- grad_tokens: bfloat16 [8192, 4096], P('ctx', 'tp')
- grad_gain: float32 [4096], P('tp')
- grad_short: float32 [3, 3, 4096], P(None, None, 'tp')
- grad_medium: float32 [128, 4096], P(None, 'tp')
- grad_skip: float32 [4096], P(('tp', 'ctx'))
- grad_residues: float32 [4096, 16], P(('tp', 'ctx'))
- grad_decay: float32 [4096, 16], P(('tp', 'ctx'))
The draws below stay inside these ranges and needn't reach their ends.
All inputs are finite; a program needn't handle non-finite values.
Results may differ from the reference program's by a relative error of at most 0.0077.
Values may be sent and summed in bfloat16 or wider, within the bound.
A program may use at most 64 MiB of HBM per device.

```python
import math
import jax
import jax.numpy as jnp
from jax import lax

D = 4096
STAP = 3
MTAP = 128
MODES = 16
SEQ = 8192


def draw_tokens(key, part):
    key_values, key_columns, key_rows = jax.random.split(key, 3)
    column_jitter = jax.random.uniform(key_columns, (D,), jnp.float32)
    row_jitter = jax.random.uniform(key_rows, (SEQ, 1), jnp.float32)
    row_scale = 10.0 ** (row_jitter * 0.5)
    column_scale = 10.0 ** (column_jitter * 0.5)
    drawn = jax.random.truncated_normal(key_values, -5.0, 5.0, (SEQ, D), jnp.float32) * 0.3
    return (drawn * column_scale * row_scale).astype(jnp.bfloat16)


def block_scale(rng, shape, cuts, smallest, largest):
    def one(dim, parts):
        steps = jax.random.uniform(jax.random.fold_in(jax.random.fold_in(rng, 6), dim), (parts,), jnp.float32, smallest / len(cuts), largest / len(cuts))
        return jnp.repeat(jnp.exp(steps), shape[dim] // parts).reshape((-1,) + (1,) * (len(shape) - dim - 1))

    gain = one(*cuts[0])
    for cut in cuts[1:]:
        gain = gain * one(*cut)
    return gain


def centred(rng, dims, spread, reach, cuts=(), kind=jnp.bfloat16):
    level = block_scale(rng, dims, cuts, -0.22, 0.18) if cuts else 1.0
    values = jax.random.normal(rng, dims, jnp.float32) * spread * level
    return jnp.minimum(jnp.maximum(values, -reach), reach).astype(kind)


def setup_inputs(seed: int = 0) -> dict:
    splits = jax.random.split(jax.random.key(seed), 9)
    return {
        "tokens": draw_tokens(jax.random.fold_in(splits[8], 71), 0),
        "norm_gain": jnp.clip(1.0 + 0.1 * jax.random.normal(splits[1], (D,), jnp.float32), 0.5, 1.5),
        "short_filter": centred(splits[2], (3, STAP, D), 0.6, 3.6, ((2, 4),), jnp.float32),
        "medium_filter": centred(splits[3], (MTAP, D), MTAP ** -0.5, 0.5, ((1, 4),), jnp.float32),
        "residues": centred(splits[4], (D, MODES), 0.35, 2.1, ((0, 256),), jnp.float32),
        "decay_rate": jnp.clip(jnp.exp(math.log(500.0) - 6.9077553 * jax.random.uniform(splits[5], (D, MODES), jnp.float32) ** block_scale(splits[5], (D, MODES), ((0, 256),), -0.2, 0.2)), 0.5, 500.0),
        "skip_gain": centred(splits[6], (D,), 1.0, 4.0, ((0, 256),), jnp.float32),
        "grad_out": centred(splits[7], (SEQ, D), 1.0, 6.0, ((0, 64), (1, 4))),
    }


EPSILON = 1e-06

def tap_sum(padded, weights, tok_rows):

    def one_tap(tap_index, running):
        where = tap_index.astype(jnp.int32)
        window = lax.dynamic_slice_in_dim(padded, where, tok_rows, 0)
        return running + weights[where] * window
    start = jnp.zeros((tok_rows, padded.shape[1]), jnp.float32)
    return lax.fori_loop(0, weights.shape[0], one_tap, start)

def lagged_sums(padded, grad_rows, taps):
    tok_rows = grad_rows.shape[0]

    def one_lag(lag_index):
        window = lax.dynamic_slice_in_dim(padded, lag_index.astype(jnp.int32), tok_rows, 0)
        return lax.optimization_barrier(jnp.sum(window * grad_rows, axis=0))
    return lax.map(one_lag, jnp.arange(taps, dtype=jnp.int32))

def long_block(block_items):
    signal, grad_rows, residues, decay_rate, skip_gain = block_items
    length = signal.shape[1]
    period = 2 * length
    mode_rates = decay_rate / length
    mode_roots = jnp.sqrt(mode_rates)
    positions = jnp.arange(length, dtype=jnp.int32).astype(jnp.float32)
    kernel = jnp.zeros(signal.shape, jnp.float32)
    for mode_index in range(residues.shape[1]):
        weight_now = residues[:, mode_index] * mode_roots[:, mode_index]
        kernel = kernel + weight_now[:, None] * jnp.exp(-mode_rates[:, mode_index, None] * positions)
    widened = signal.astype(jnp.float32)
    grad_wide = grad_rows.astype(jnp.float32)
    spec_signal = jnp.fft.rfft(widened, n=period, axis=1)
    spec_kernel = jnp.fft.rfft(kernel, n=period, axis=1)
    spec_grad = jnp.fft.rfft(grad_wide, n=period, axis=1)
    conv_part = jnp.fft.irfft(spec_signal * spec_kernel, n=period, axis=1)[:, :length]
    result = (conv_part + skip_gain[:, None] * widened).astype(jnp.bfloat16)
    back_part = jnp.fft.irfft(jnp.conj(spec_kernel) * spec_grad, n=period, axis=1)[:, :length]
    back_rows = (back_part + skip_gain[:, None] * grad_wide).astype(jnp.bfloat16)
    kernel_grad = jnp.fft.irfft(jnp.conj(spec_signal) * spec_grad, n=period, axis=1)[:, :length]
    grad_skip = lax.optimization_barrier(jnp.sum(grad_wide * widened, axis=1))
    first_list = []
    second_list = []
    for mode_index in range(residues.shape[1]):
        decayed = jnp.exp(-mode_rates[:, mode_index, None] * positions)
        first_list.append(lax.optimization_barrier(jnp.sum(kernel_grad * decayed, axis=1)))
        second_list.append(lax.optimization_barrier(jnp.sum(kernel_grad * decayed * positions, axis=1)))
    first_sum = jnp.stack(first_list, 1)
    second_sum = jnp.stack(second_list, 1)
    grad_residues = mode_roots * first_sum
    grad_decay = residues / length * (first_sum / (2.0 * mode_roots) - mode_roots * second_sum)
    return (result, back_rows, grad_skip, grad_residues, grad_decay)

def reference(tokens, norm_gain, short_filter, medium_filter, residues, decay_rate, skip_gain, grad_out):
    tok_rows = tokens.shape[0]
    channels = tokens.shape[1]
    short_taps = short_filter.shape[1]
    long_taps = medium_filter.shape[0]
    widened = tokens.astype(jnp.float32)
    inv_rms = lax.rsqrt(lax.optimization_barrier(jnp.sum(widened * widened, axis=1)) / channels + EPSILON)
    normed = (widened * inv_rms[:, None] * norm_gain).astype(jnp.bfloat16)
    normed_ext = jnp.concatenate([jnp.zeros((short_taps - 1, channels), jnp.bfloat16), normed], 0).astype(jnp.float32)
    query_rows = tap_sum(normed_ext, short_filter[0][::-1], tok_rows)
    key_rows = tap_sum(normed_ext, short_filter[1][::-1], tok_rows)
    value_rows = tap_sum(normed_ext, short_filter[2][::-1], tok_rows)
    gated = (key_rows * value_rows).astype(jnp.bfloat16)
    gated_ext = jnp.concatenate([jnp.zeros((long_taps - 1, channels), jnp.bfloat16), gated], 0).astype(jnp.float32)
    signal = tap_sum(gated_ext, medium_filter[::-1], tok_rows).astype(jnp.bfloat16)
    grad_gate = (grad_out.astype(jnp.float32) * query_rows).astype(jnp.bfloat16)
    group_count = channels // 256
    block_items = (signal.T.reshape(group_count, 256, tok_rows), grad_gate.T.reshape(group_count, 256, tok_rows), residues.reshape(group_count, 256, residues.shape[1]), decay_rate.reshape(group_count, 256, residues.shape[1]), skip_gain.reshape(group_count, 256))
    result, back_cols, grad_skip, grad_residues, grad_decay = lax.map(long_block, block_items)
    conv_rows = result.reshape(channels, tok_rows).T
    back_rows = back_cols.reshape(channels, tok_rows).T
    conv_wide = conv_rows.astype(jnp.float32)
    block_out = (query_rows * conv_wide).astype(jnp.bfloat16)
    grad_query = grad_out.astype(jnp.float32) * conv_wide
    back_ext = jnp.concatenate([back_rows, jnp.zeros((long_taps - 1, channels), jnp.bfloat16)], 0).astype(jnp.float32)
    grad_gated = tap_sum(back_ext, medium_filter, tok_rows)
    grad_medium = lagged_sums(gated_ext, back_rows.astype(jnp.float32), long_taps)[::-1]
    streams = [grad_query.astype(jnp.bfloat16), (grad_gated * value_rows).astype(jnp.bfloat16), (grad_gated * key_rows).astype(jnp.bfloat16)]
    grad_normed = jnp.zeros((tok_rows, channels), jnp.float32)
    short_list = []
    for stream_index in range(3):
        stream_ext = jnp.concatenate([streams[stream_index], jnp.zeros((short_taps - 1, channels), jnp.bfloat16)], 0).astype(jnp.float32)
        grad_normed = grad_normed + tap_sum(stream_ext, short_filter[stream_index], tok_rows)
        short_list.append(lagged_sums(normed_ext, streams[stream_index].astype(jnp.float32), short_taps)[::-1])
    grad_short = jnp.stack(short_list, 0)
    grad_gain = lax.optimization_barrier(jnp.sum(grad_normed * widened * inv_rms[:, None], axis=0))
    scaled = grad_normed * norm_gain
    dot_sums = lax.optimization_barrier(jnp.sum(scaled * widened, axis=1))
    cubed = inv_rms * inv_rms * inv_rms
    grad_tokens = (inv_rms[:, None] * scaled - widened * (cubed * dot_sums / channels)[:, None]).astype(jnp.bfloat16)
    return (block_out, grad_tokens, grad_gain, grad_short, grad_medium, grad_skip.reshape(channels), grad_residues.reshape(channels, residues.shape[1]), grad_decay.reshape(channels, residues.shape[1]))
```

```python
import functools
import math

import jax
import jax.numpy as jnp
from jax import lax
from jax.experimental import pallas as pl
from jax.experimental.pallas import tpu as pltpu
from jax.sharding import PartitionSpec as P

EPSILON = 1e-06
HIGHEST = lax.Precision.HIGHEST
radix_cols = 128


def tile_of(index, lane_blocks):
    rows = pl.multiple_of((index // lane_blocks) * 16, 16)
    lanes = pl.multiple_of((index % lane_blocks) * 128, 128)
    return (pl.ds(rows, 16), pl.ds(lanes, 128))


def grad_sum_kernel(n, tiles_ref, rows_ref, tiles_out, rows_out, tiles_in, rows_in, tile_red, row_red,
                    tile_send, tile_recv, row_send, row_recv, tile_send2, tile_recv2, row_send2, row_recv2):
    me = lax.axis_index("ctx")
    lane_blocks = tiles_ref.shape[1] // 128
    barrier = pltpu.get_barrier_semaphore()

    def greet(d, carry):
        pl.semaphore_signal(barrier, inc=1, device_id={"ctx": lax.rem(me + d, n)}, device_id_type=pl.DeviceIdType.MESH)
        return carry

    lax.fori_loop(1, n, greet, 0)
    pl.semaphore_wait(barrier, n - 1)

    def scatter(d):
        peer = lax.rem(me + d, n)
        return (
            pltpu.make_async_remote_copy(tiles_ref.at[tile_of(peer, lane_blocks)], tiles_in.at[d], tile_send.at[d], tile_recv.at[d],
                                         device_id={"ctx": peer}, device_id_type=pl.DeviceIdType.MESH),
            pltpu.make_async_remote_copy(rows_ref.at[peer], rows_in.at[d], row_send.at[d], row_recv.at[d],
                                         device_id={"ctx": peer}, device_id_type=pl.DeviceIdType.MESH),
        )

    def gather(d):
        peer = lax.rem(me + d, n)
        return (
            pltpu.make_async_remote_copy(tile_red, tiles_out.at[tile_of(me, lane_blocks)], tile_send2.at[d], tile_recv2.at[d],
                                         device_id={"ctx": peer}, device_id_type=pl.DeviceIdType.MESH),
            pltpu.make_async_remote_copy(row_red, rows_out.at[me], row_send2.at[d], row_recv2.at[d],
                                         device_id={"ctx": peer}, device_id_type=pl.DeviceIdType.MESH),
        )

    def start_all(make):
        def body(d, carry):
            for copy in make(d):
                copy.start()
            return carry

        lax.fori_loop(1, n, body, 0)

    start_all(scatter)

    def add(d, totals):
        first, second = scatter(d)
        first.wait_recv()
        second.wait_recv()
        return (totals[0] + tiles_in[d].astype(jnp.float32), totals[1] + rows_in[d])

    own = tile_of(me, lane_blocks)
    tile_total, row_total = lax.fori_loop(1, n, add, (tiles_ref[own].astype(jnp.float32), rows_ref[me]))
    tile_red[...] = tile_total.astype(jnp.bfloat16)
    row_red[...] = row_total
    start_all(gather)
    tiles_out[own] = tile_total.astype(jnp.bfloat16)
    rows_out[me] = row_total

    def finish(d, carry):
        for copy in gather(d):
            copy.wait()
        for copy in scatter(d):
            copy.wait_send()
        return carry

    lax.fori_loop(1, n, finish, 0)


def sum_over_ctx(tiles, rows):
    n = lax.axis_size("ctx")
    sems = [pltpu.SemaphoreType.DMA((n,))] * 8
    return pl.pallas_call(
        functools.partial(grad_sum_kernel, n),
        out_shape=(jax.ShapeDtypeStruct(tiles.shape, jnp.bfloat16), jax.ShapeDtypeStruct(rows.shape, jnp.float32)),
        in_specs=[pl.BlockSpec(memory_space=pltpu.VMEM)] * 2,
        out_specs=[pl.BlockSpec(memory_space=pltpu.VMEM)] * 2,
        scratch_shapes=[
            pltpu.VMEM((n, 16, 128), jnp.bfloat16),
            pltpu.VMEM((n,) + rows.shape[1:], jnp.float32),
            pltpu.VMEM((16, 128), jnp.bfloat16),
            pltpu.VMEM(rows.shape[1:], jnp.float32),
        ] + sems,
        compiler_params=pltpu.CompilerParams(collective_id=7, has_side_effects=True),
    )(tiles, rows)


def from_behind(shard, axis, by):
    devices = lax.axis_size(axis)
    pairs = [(i, i + by) for i in range(devices) if 0 <= i + by < devices]
    return lax.ppermute(shard, axis, pairs)


def depthwise(extended, weights):
    result = lax.conv_general_dilated(
        extended[None],
        weights[:, None, :],
        (1,),
        "VALID",
        dimension_numbers=("NWC", "WIO", "NWC"),
        feature_group_count=extended.shape[1],
        precision=HIGHEST,
    )
    return result[0]


def angle_tables(count, other, period):
    first_index = lax.broadcasted_iota(jnp.int32, (count, other), 0)
    second_index = lax.broadcasted_iota(jnp.int32, (count, other), 1)
    angles = (first_index * second_index % period).astype(jnp.float32) * (2.0 * math.pi / period)
    return (jnp.cos(angles), jnp.sin(angles))


def contract(pattern, operand, matrix):
    return jnp.einsum(
        pattern, operand, matrix, precision=HIGHEST, preferred_element_type=jnp.float32
    )


def forward_spectrum(signal):
    channels = signal.shape[0]
    length = signal.shape[1]
    period = 2 * length
    spectrum_rows = period // radix_cols
    half_rows = spectrum_rows // 2
    blocked = signal.reshape(channels, half_rows, radix_cols)
    cos_outer, sin_outer = angle_tables(half_rows, spectrum_rows, spectrum_rows)
    section_real = contract("cab,ak->ckb", blocked, cos_outer)
    section_imag = -contract("cab,ak->ckb", blocked, sin_outer)
    cos_twist, sin_twist = angle_tables(spectrum_rows, radix_cols, period)
    twist_real = section_real * cos_twist + section_imag * sin_twist
    twist_imag = section_imag * cos_twist - section_real * sin_twist
    cos_inner, sin_inner = angle_tables(radix_cols, radix_cols, radix_cols)
    spec_real = contract("ckb,bm->ckm", twist_real, cos_inner) + contract(
        "ckb,bm->ckm", twist_imag, sin_inner
    )
    spec_imag = contract("ckb,bm->ckm", twist_imag, cos_inner) - contract(
        "ckb,bm->ckm", twist_real, sin_inner
    )
    return (spec_real, spec_imag)


def inverse_spectrum(spec_real, spec_imag):
    channels = spec_real.shape[0]
    spectrum_rows = spec_real.shape[1]
    period = spectrum_rows * radix_cols
    half_rows = spectrum_rows // 2
    cos_inner, sin_inner = angle_tables(radix_cols, radix_cols, radix_cols)
    mid_real = contract("ckm,mb->ckb", spec_real, cos_inner) - contract(
        "ckm,mb->ckb", spec_imag, sin_inner
    )
    mid_imag = contract("ckm,mb->ckb", spec_imag, cos_inner) + contract(
        "ckm,mb->ckb", spec_real, sin_inner
    )
    cos_twist, sin_twist = angle_tables(spectrum_rows, radix_cols, period)
    twist_real = mid_real * cos_twist - mid_imag * sin_twist
    twist_imag = mid_imag * cos_twist + mid_real * sin_twist
    cos_outer, sin_outer = angle_tables(spectrum_rows, half_rows, spectrum_rows)
    result = contract("ckb,ka->cab", twist_real, cos_outer) - contract(
        "ckb,ka->cab", twist_imag, sin_outer
    )
    return result.reshape(channels, half_rows * radix_cols) / period


def long_forward(signal, residues, decay_rate, skip_gain):
    length = signal.shape[1]
    mode_rates = decay_rate / length
    mode_roots = jnp.sqrt(mode_rates)
    positions = jnp.arange(length, dtype=jnp.int32).astype(jnp.float32)
    kernel = jnp.zeros(signal.shape, jnp.float32)
    for mode_index in range(residues.shape[1]):
        weight_now = residues[:, mode_index] * mode_roots[:, mode_index]
        kernel = kernel + weight_now[:, None] * jnp.exp(
            -mode_rates[:, mode_index, None] * positions
        )
    widened = signal.astype(jnp.float32)
    sig_real, sig_imag = forward_spectrum(widened)
    ker_real, ker_imag = forward_spectrum(kernel)
    conv_part = inverse_spectrum(
        sig_real * ker_real - sig_imag * ker_imag, sig_real * ker_imag + sig_imag * ker_real
    )
    result = (conv_part + skip_gain[:, None] * widened).astype(jnp.bfloat16)
    return (result, (widened, sig_real, sig_imag, ker_real, ker_imag))


def long_backward(grad_cols, saved, residues, decay_rate, skip_gain):
    widened, sig_real, sig_imag, ker_real, ker_imag = saved
    length = grad_cols.shape[1]
    mode_rates = decay_rate / length
    mode_roots = jnp.sqrt(mode_rates)
    positions = jnp.arange(length, dtype=jnp.int32).astype(jnp.float32)
    grad_wide = grad_cols.astype(jnp.float32)
    grad_real, grad_imag = forward_spectrum(grad_wide)
    back_part = inverse_spectrum(
        ker_real * grad_real + ker_imag * grad_imag, ker_real * grad_imag - ker_imag * grad_real
    )
    back_cols = (back_part + skip_gain[:, None] * grad_wide).astype(jnp.bfloat16)
    kernel_grad = inverse_spectrum(
        sig_real * grad_real + sig_imag * grad_imag, sig_real * grad_imag - sig_imag * grad_real
    )
    grad_skip = jnp.sum(grad_wide * widened, axis=1)
    first_list = []
    second_list = []
    for mode_index in range(residues.shape[1]):
        decayed = kernel_grad * jnp.exp(-mode_rates[:, mode_index, None] * positions)
        first_list.append(jnp.sum(decayed, axis=1))
        second_list.append(jnp.sum(decayed * positions, axis=1))
    first_sum = jnp.stack(first_list, 1)
    second_sum = jnp.stack(second_list, 1)
    grad_residues = mode_roots * first_sum
    grad_decay = residues / length * (first_sum / (2.0 * mode_roots) - mode_roots * second_sum)
    return (back_cols, grad_skip, grad_residues, grad_decay)


def per_device(
    tokens, norm_gain, short_filter, medium_filter, residues, decay_rate, skip_gain, grad_out
):
    tok_rows = tokens.shape[0]
    channels = tokens.shape[1]
    short_taps = short_filter.shape[1]
    long_taps = medium_filter.shape[0]
    total_chans = channels * lax.axis_size("tp")
    widened = tokens.astype(jnp.float32)
    squares = lax.psum(jnp.sum(widened * widened, axis=1), "tp")
    inv_rms = lax.rsqrt(squares / total_chans + EPSILON)
    normed = (widened * inv_rms[:, None] * norm_gain).astype(jnp.bfloat16)
    filter_bank = short_filter.transpose(1, 0, 2).reshape(short_taps, 3 * channels)
    rim_before = from_behind(normed[tok_rows - short_taps + 1 :], "ctx", 1)
    normed_window = jnp.concatenate([rim_before, normed], 0).astype(jnp.float32)
    mixed_rows = depthwise(jnp.tile(normed_window, (1, 3)), filter_bank[::-1])
    query_rows = mixed_rows[:, :channels]
    key_rows = mixed_rows[:, channels : 2 * channels]
    value_rows = mixed_rows[:, 2 * channels :]
    gated = (key_rows * value_rows).astype(jnp.bfloat16)
    gated_before = from_behind(gated[tok_rows - long_taps + 1 :], "ctx", 1)
    gated_ext = jnp.concatenate([gated_before, gated], 0)
    gated_wide = gated_ext.astype(jnp.float32)
    signal = depthwise(gated_wide, medium_filter[::-1]).astype(jnp.bfloat16)
    grad_gate = (grad_out.astype(jnp.float32) * query_rows).astype(jnp.bfloat16)
    signal_cols = lax.all_to_all(signal.T, "ctx", split_axis=0, concat_axis=1, tiled=True)
    conv_cols, saved = long_forward(signal_cols, residues, decay_rate, skip_gain)
    conv_back = lax.all_to_all(conv_cols, "ctx", split_axis=1, concat_axis=0, tiled=True)
    grad_cols = lax.all_to_all(grad_gate.T, "ctx", split_axis=0, concat_axis=1, tiled=True)
    back_cols, grad_skip, grad_residues, grad_decay = long_backward(
        grad_cols, saved, residues, decay_rate, skip_gain
    )
    back_back = lax.all_to_all(back_cols, "ctx", split_axis=1, concat_axis=0, tiled=True)
    conv_wide = conv_back.T.astype(jnp.float32)
    block_out = (query_rows * conv_wide).astype(jnp.bfloat16)
    grad_query = grad_out.astype(jnp.float32) * conv_wide
    back_rows = back_back.T
    back_after = from_behind(back_rows[: long_taps - 1], "ctx", -1)
    grad_gated = depthwise(
        jnp.concatenate([back_rows, back_after], 0).astype(jnp.float32), medium_filter
    )
    grad_medium_part = depthwise(gated_wide, back_rows.astype(jnp.float32))[::-1]
    streams = jnp.concatenate(
        [grad_query, grad_gated * value_rows, grad_gated * key_rows], 1
    ).astype(jnp.bfloat16)
    stream_after = from_behind(streams[: short_taps - 1], "ctx", -1)
    grad_three = depthwise(
        jnp.concatenate([streams, stream_after], 0).astype(jnp.float32), filter_bank
    )
    grad_normed = (
        grad_three[:, :channels]
        + grad_three[:, channels : 2 * channels]
        + grad_three[:, 2 * channels :]
    )
    short_lagged = depthwise(jnp.tile(normed_window, (1, 3)), streams.astype(jnp.float32))[::-1]
    grad_short_part = short_lagged.reshape(short_taps, 3, channels).transpose(1, 0, 2)
    grad_gain_part = jnp.sum(grad_normed * widened * inv_rms[:, None], axis=0)
    n = lax.axis_size("ctx")
    small = jnp.concatenate([grad_short_part.reshape(9, channels), grad_gain_part[None]], 0).reshape(-1, 128)
    small = jnp.pad(small, ((0, 2 * n - small.shape[0]), (0, 0))).reshape(n, 2, 128)
    medium_sum, small_sum = sum_over_ctx(grad_medium_part.astype(jnp.bfloat16), small)
    grad_medium = medium_sum.astype(jnp.float32)
    small_rows = small_sum.reshape(2 * n, 128)[: 10 * (channels // 128)].reshape(10, channels)
    grad_short = small_rows[:9].reshape(3, 3, channels)
    grad_gain = small_rows[9]
    scaled = grad_normed * norm_gain
    dot_sums = lax.psum(jnp.sum(scaled * widened, axis=1), "tp")
    cubed = inv_rms * inv_rms * inv_rms
    grad_tokens = (
        inv_rms[:, None] * scaled - widened * (cubed * dot_sums / total_chans)[:, None]
    ).astype(jnp.bfloat16)
    return (
        block_out,
        grad_tokens,
        grad_gain,
        grad_short,
        grad_medium,
        grad_skip,
        grad_residues,
        grad_decay,
    )


def solution(mesh):
    in_specs = (
        P("ctx", "tp"),
        P("tp"),
        P(None, None, "tp"),
        P(None, "tp"),
        P(("tp", "ctx"), None),
        P(("tp", "ctx"), None),
        P(("tp", "ctx")),
        P("ctx", "tp"),
    )
    out_specs = (
        P("ctx", "tp"),
        P("ctx", "tp"),
        P("tp"),
        P(None, None, "tp"),
        P(None, "tp"),
        P(("tp", "ctx")),
        P(("tp", "ctx"), None),
        P(("tp", "ctx"), None),
    )
    return jax.shard_map(
        per_device, mesh=mesh, in_specs=in_specs, out_specs=out_specs, check_vma=False
    )
```

```python
import functools
import math

import jax
import jax.numpy as jnp
import ml_dtypes
import numpy as np
from jax import lax
from jax.experimental import pallas as pl
from jax.experimental.pallas import tpu as pltpu
from jax.sharding import PartitionSpec as P

EPSILON = 1e-06
HIGHEST = lax.Precision.HIGHEST
MESH = pl.DeviceIdType.MESH
TOK = 128
MODES = 16
LANES = 128
f32 = jnp.float32
bf16 = jnp.bfloat16
VMEM_SPEC = pl.BlockSpec(memory_space=pltpu.VMEM)


def transform_tables():
    freq = 2 * np.arange(TOK)[:, None] + 1
    angle = np.pi / 256.0 * ((freq * np.arange(256)[None, :]) % 512)
    table = np.concatenate([np.cos(angle), -np.sin(angle)], 0)

    def two(matrix):
        high = matrix.astype(ml_dtypes.bfloat16)
        return high, (matrix - high.astype(np.float64)).astype(ml_dtypes.bfloat16)

    high, low = two(table)
    near, far = slice(0, TOK), slice(TOK, 256)
    inv_near, inv_near_low = two(table[:, near].T / 128.0)
    inv_far, inv_far_low = two(table[:, far].T / 128.0)
    cat = lambda *parts: np.concatenate(parts, 1)
    return {
        "whole2": cat(high, low),
        "near2": cat(high[:, near], low[:, near]),
        "far2": cat(high[:, far], low[:, far]),
        "near3": cat(high[:, near], high[:, near], low[:, near]),
        "inv_near3": cat(inv_near, inv_near, inv_near_low),
        "inv_far3": cat(inv_far, inv_far, inv_far_low),
    }


def lane_orders():
    order = np.zeros((2, 64, LANES), np.float32)
    for half in range(2):
        for row in range(64):
            order[half, row, 16 * (row // 8) + 8 * half + row % 8] = 1.0
    return order


def dot2(table, data):
    return jnp.dot(table, jnp.concatenate([data, data], 0), preferred_element_type=f32)


def dot3(table, data):
    high = data.astype(bf16)
    low = (data - high.astype(f32)).astype(bf16)
    return jnp.dot(table, jnp.concatenate([high, low, high], 0), preferred_element_type=f32)


def halves(spectrum):
    return spectrum[:TOK], spectrum[TOK:]


def product(first, second):
    (a, b), (c, d) = halves(first), halves(second)
    return jnp.concatenate([a * c - b * d, a * d + b * c], 0)


def product_conj(first, second):
    (a, b), (c, d) = halves(first), halves(second)
    return jnp.concatenate([a * c + b * d, b * c - a * d], 0)


def eye(size):
    return (lax.broadcasted_iota(jnp.int32, (size, size), 0) == lax.broadcasted_iota(jnp.int32, (size, size), 1)).astype(f32)


def to_column(row):
    return jnp.sum(eye(row.shape[1]) * row, axis=1, keepdims=True)


def to_row(column):
    return jnp.sum(eye(column.shape[0]) * column, axis=0, keepdims=True)


def place(row, step, part, lane_blocks):
    if lane_blocks == 1:
        return row // 2, row % 2
    return row * (lane_blocks // 2) + step, part


def greet(barrier, count, axis, skip=0):
    me = lax.axis_index(axis)

    def body(d, carry):
        pl.semaphore_signal(barrier, inc=1, device_id={axis: lax.rem(me + d, count)}, device_id_type=MESH)
        return carry

    lax.fori_loop(1, count, body, 0)


def send(src, dst, send_sem, recv_sem, **where):
    return pltpu.make_async_remote_copy(src, dst, send_sem, recv_sem, device_id=where, device_id_type=MESH)


def each(first, last, work):
    def body(d, carry):
        work(d)
        return carry

    lax.fori_loop(first, last, body, 0)


def entry_kernel(n, n_tp, total, tok_ref, res_ref, rate_ref, skip_ref,
                 inv_ref, prev_ref, prev2_ref, par_ref,
                 msg, sums, sums_in, inv_own, psend, precv, tsend, trecv, ssend, srecv, isend, irecv):
    me = lax.axis_index("ctx")
    tp = lax.axis_index("tp")
    barrier = pltpu.get_barrier_semaphore()
    greet(barrier, n, "ctx")
    greet(barrier, n_tp, "tp")
    length = n * TOK
    msg[...] = jnp.zeros(msg.shape, f32)
    msg[:, 0:16] = res_ref[0:8, :]
    msg[:, 16:32] = res_ref[8:16, :]
    msg[:, 32:48] = rate_ref[0:8, :] / length
    msg[:, 48:64] = rate_ref[8:16, :] / length
    skip_col = to_column(skip_ref[...])
    msg[:, 64:65] = skip_col[0:8]
    msg[:, 65:66] = skip_col[8:16]
    wide = tok_ref[...].astype(f32)
    sums[...] = jnp.broadcast_to(to_row(jnp.sum(wide * wide, axis=1, keepdims=True)), sums.shape)
    pl.semaphore_wait(barrier, n - 1 + n_tp - 1)

    def sum_copy(d):
        return send(sums, sums_in.at[d], ssend.at[d], srecv.at[d], tp=lax.rem(tp + d, n_tp))

    def par_copy(d):
        return send(msg, par_ref.at[me], psend.at[d], precv.at[d], ctx=lax.rem(me + d, n))

    one = lax.rem(me + 1, n)
    two = lax.rem(me + 2, n)
    tok_copy = send(tok_ref, prev_ref, tsend.at[0], trecv.at[0], ctx=one)
    tail_copy = send(tok_ref.at[pl.ds(TOK - 16, 16)], prev2_ref, tsend.at[1], trecv.at[1], ctx=two)
    for d in range(1, n_tp):
        sum_copy(d).start()
    tail_copy.start()
    tok_copy.start()
    each(1, n, lambda d: par_copy(d).start())
    par_ref[me] = msg[...]
    squares = sums[...]
    for d in range(1, n_tp):
        sum_copy(d).wait_recv()
        squares = squares + sums_in[d]
    inv_own[...] = lax.rsqrt(squares / total + EPSILON)
    inv_copies = [
        send(inv_own, inv_ref.at[1], isend.at[0], irecv.at[0], ctx=one),
        send(inv_own, inv_ref.at[2], isend.at[1], irecv.at[1], ctx=two),
    ]
    for copy in inv_copies:
        copy.start()
    inv_ref[0] = inv_own[...]
    for copy in inv_copies + [tok_copy, tail_copy]:
        copy.wait()
    for d in range(1, n_tp):
        sum_copy(d).wait_send()
    each(1, n, lambda d: par_copy(d).wait())


def entry(tokens, residues, decay_rate, skip_gain, total):
    n, n_tp = lax.axis_size("ctx"), lax.axis_size("tp")
    channels = tokens.shape[1]
    dma = pltpu.SemaphoreType.DMA
    return pl.pallas_call(
        functools.partial(entry_kernel, n, n_tp, total),
        out_shape=(
            jax.ShapeDtypeStruct((3, 8, TOK), f32),
            jax.ShapeDtypeStruct((TOK, channels), bf16),
            jax.ShapeDtypeStruct((16, channels), bf16),
            jax.ShapeDtypeStruct((n, 8, LANES), f32),
        ),
        in_specs=[VMEM_SPEC] * 4,
        out_specs=[VMEM_SPEC] * 4,
        scratch_shapes=[
            pltpu.VMEM((8, LANES), f32), pltpu.VMEM((8, TOK), f32), pltpu.VMEM((n_tp, 8, TOK), f32), pltpu.VMEM((8, TOK), f32),
            dma((n,)), dma((n,)), dma((2,)), dma((2,)), dma((n_tp,)), dma((n_tp,)), dma((2,)), dma((2,)),
        ],
        compiler_params=pltpu.CompilerParams(collective_id=1, has_side_effects=True),
        name="entry",
    )(tokens, residues, decay_rate, skip_gain.reshape(1, -1))


def powers(rate_row, exponents):
    return jnp.exp(-rate_row * exponents)


def sublanes():
    return lax.broadcasted_iota(jnp.int32, (8, LANES), 0).astype(f32)


def horner(blocks, eighth):
    total = blocks[-1]
    moment = jnp.zeros_like(total)
    for block in blocks[-2::-1]:
        shifted = eighth * total
        moment = eighth * moment + shifted
        total = shifted + block
    return total, moment


def down(values):
    return jnp.sum(values, axis=0, keepdims=True)


def forward_kernel(n, lane_blocks, inv_ref, tok_ref, prev_ref, prev2_ref, gain_ref, sf_ref, mf_ref, par_ref, gout_ref,
                   order_ref, whole2, near2, near3, inv_near3, inv_far3,
                   q_ref, k_ref, v_ref, normed_ref, gspec_ref, mspec_ref, conv_ref, back_ref, gskip_ref,
                   sr_ref, aux_ref, rows_ref, ext, kern, sig, grd, kgr):
    step = pl.program_id(0)
    width = tok_ref.shape[1]
    me = lax.axis_index("ctx")
    gain = gain_ref[...]

    def normed_of(values, inv_row, live):
        scale = to_column(inv_row)[TOK - values.shape[0]:]
        rounded = (values.astype(f32) * scale * gain).astype(bf16).astype(f32)
        return jnp.where(live, rounded, 0.0)

    ext[0:16] = normed_of(prev2_ref[...], inv_ref[2, 0:1], me >= 2)
    ext[16:144] = normed_of(prev_ref[...], inv_ref[1, 0:1], me >= 1)
    ext[144:272] = normed_of(tok_ref[...], inv_ref[0, 0:1], me >= 0)
    normed_ref[...] = ext[136:272]

    def stream(s, first, count):
        total = sf_ref[3 * s:3 * s + 1] * ext[first:first + count]
        for j in range(1, 3):
            total = total + sf_ref[3 * s + j:3 * s + j + 1] * ext[first - j:first - j + count]
        return total

    query = stream(0, 144, TOK)
    q_ref[...] = query
    keys = stream(1, 16, 256)
    values = stream(2, 16, 256)
    k_ref[...] = keys[TOK:]
    v_ref[...] = values[TOK:]
    gated = (keys * values).astype(bf16)
    gspec = dot2(whole2[...], gated)
    mspec = dot3(near3[...], mf_ref[...])
    gspec_ref[...] = gspec
    mspec_ref[...] = mspec
    signal = dot3(inv_far3[...], product(gspec, mspec)).astype(bf16)
    grad_gate = (gout_ref[...].astype(f32) * query).astype(bf16)
    sig[...] = signal.astype(f32)
    grd[...] = grad_gate.astype(f32)
    gskip_ref[...] = down(sig[...] * grd[...])

    r = sublanes()
    tables = []
    for part in range(width // LANES):
        lanes = slice(part * LANES, (part + 1) * LANES)
        packed = par_ref[8 * part:8 * part + 8].reshape(64, LANES).T
        even = jnp.dot(packed, order_ref[0], precision=HIGHEST, preferred_element_type=f32)
        odd = jnp.dot(packed, order_ref[1], precision=HIGHEST, preferred_element_type=f32)
        res = even[0:16] + odd[16:32]
        rate = even[32:48] + odd[48:64]
        skip = even[64:65] + odd[65:66]
        weight = res * jnp.sqrt(rate)
        eighths = []
        running = []
        for m in range(MODES):
            eighths.append(jnp.broadcast_to(jnp.exp(-8.0 * rate[m:m + 1]), (8, LANES)))
            running.append(weight[m:m + 1] * powers(rate[m:m + 1], r))
            piece, row = place(m, step, part, lane_blocks)
            rows_ref[piece, pl.ds(row, 1)] = res[m:m + 1]
            rows_ref[piece, pl.ds(2 + row, 1)] = rate[m:m + 1]
            rows_ref[piece, pl.ds(4 + row, 1)] = jnp.exp(-float(TOK) * rate[m:m + 1])
        for block in range(16):
            total = running[0]
            for m in range(1, MODES):
                total = total + running[m]
            if block == 0:
                total = total + jnp.where(r == 0.0, skip, 0.0)
            kern[8 * block:8 * block + 8, lanes] = total
            running = [value * eighth for value, eighth in zip(running, eighths)]
        tables.append((rate, eighths))
    kspec = dot3(near3[...], kern[...])
    uspec = dot2(near2[...], signal)
    cspec = dot2(near2[...], grad_gate)
    conv_ref[...] = dot3(inv_near3[...], product(kspec, uspec))
    back_ref[...] = dot3(inv_near3[...], product_conj(cspec, kspec))
    kgr[...] = dot3(inv_near3[...], product_conj(cspec, uspec))
    for part in range(width // LANES):
        lanes = slice(part * LANES, (part + 1) * LANES)
        rate, eighths = tables[part]
        for m in range(MODES):
            piece, row = place(m, step, part, lane_blocks)
            rising = powers(rate[m:m + 1], r)
            falling = powers(rate[m:m + 1], 7.0 - r)
            load = lambda ref: [ref[8 * b:8 * b + 8, lanes] for b in range(16)]
            total, moment = horner(load(sig)[::-1], eighths[m])
            sr_ref[piece, pl.ds(row, 1)] = down(falling * total)
            aux_ref[piece, pl.ds(row, 1)] = down(falling * (8.0 * moment + (7.0 - r) * total))
            total, moment = horner(load(grd), eighths[m])
            sr_ref[piece, pl.ds(2 + row, 1)] = down(rising * total)
            aux_ref[piece, pl.ds(2 + row, 1)] = down(rising * (8.0 * moment + r * total))
            total, moment = horner(load(kgr), eighths[m])
            aux_ref[piece, pl.ds(4 + row, 1)] = down(rising * total)
            aux_ref[piece, pl.ds(6 + row, 1)] = down(rising * (8.0 * moment + r * total))


def split_lanes(rows, width):
    return pl.BlockSpec((rows, width), lambda i: (0, i))


def whole(*shape):
    return pl.BlockSpec(shape, lambda i: (0,) * len(shape))


def block_width(channels):
    return min(256, channels)


def forward(inv, tokens, prev, prev2, gain, short, medium, par, grad_out, tables, order):
    channels = tokens.shape[1]
    width = block_width(channels)
    n = par.shape[0]
    lane_blocks = channels // LANES
    lanes = lambda rows: split_lanes(rows, width)
    names = ("whole2", "near2", "near3", "inv_near3", "inv_far3")
    mats = [tables[name] for name in names]
    wide = lambda rows: jax.ShapeDtypeStruct((rows, channels), f32)
    return pl.pallas_call(
        functools.partial(forward_kernel, n, lane_blocks),
        grid=(channels // width,),
        out_shape=(wide(TOK), wide(TOK), wide(TOK), wide(136), wide(256), wide(256), wide(TOK), wide(TOK), wide(1),
                   jax.ShapeDtypeStruct((n, 4, LANES), f32), jax.ShapeDtypeStruct((n, 8, LANES), f32), jax.ShapeDtypeStruct((n, 8, LANES), f32)),
        in_specs=[whole(3, 8, TOK), lanes(TOK), lanes(TOK), lanes(16), lanes(1), lanes(9), lanes(TOK),
                  pl.BlockSpec((8 * width // LANES, 8, LANES), lambda i: (i, 0, 0)), lanes(TOK), whole(2, 64, LANES)]
        + [whole(*mat.shape) for mat in mats],
        out_specs=[lanes(TOK), lanes(TOK), lanes(TOK), lanes(136), lanes(256), lanes(256), lanes(TOK), lanes(TOK), lanes(1),
                   whole(n, 4, LANES), whole(n, 8, LANES), whole(n, 8, LANES)],
        scratch_shapes=[pltpu.VMEM((272, width), f32)] + [pltpu.VMEM((TOK, width), f32)] * 4,
        name="forward",
    )(inv, tokens, prev, prev2, gain, short, medium, par, grad_out, order, *mats)


def states_kernel(n, sr_ref, rows_ref, hq_ref, inbox, outbox, send1, recv1, send2, recv2):
    me = lax.axis_index("ctx")
    barrier = pltpu.get_barrier_semaphore()
    greet(barrier, n, "ctx")
    pl.semaphore_wait(barrier, n - 1)

    def out_copy(d):
        peer = lax.rem(me + d, n)
        return send(sr_ref.at[peer], inbox.at[me], send1.at[d], recv1.at[d], ctx=peer)

    def back_copy(d):
        peer = lax.rem(me + d, n)
        return send(outbox.at[peer], hq_ref.at[me], send2.at[d], recv2.at[d], ctx=peer)

    each(1, n, lambda d: out_copy(d).start())
    inbox[me] = sr_ref[me]
    decay = rows_ref[me][4:6]
    each(1, n, lambda d: out_copy(d).wait())

    def scan(i, carry):
        ahead, behind = carry
        j = n - 1 - i
        outbox[i, 0:2] = ahead
        outbox[j, 2:4] = behind
        return decay * ahead + inbox[i][0:2], decay * behind + inbox[j][2:4]

    zero = jnp.zeros((2, LANES), f32)
    lax.fori_loop(0, n, scan, (zero, zero))
    each(1, n, lambda d: back_copy(d).start())
    hq_ref[me] = outbox[me]
    each(1, n, lambda d: back_copy(d).wait())


def states(sr, rows):
    n = sr.shape[0]
    dma = pltpu.SemaphoreType.DMA
    return pl.pallas_call(
        functools.partial(states_kernel, n),
        out_shape=jax.ShapeDtypeStruct(sr.shape, f32),
        in_specs=[VMEM_SPEC] * 2,
        out_specs=VMEM_SPEC,
        scratch_shapes=[pltpu.VMEM(sr.shape, f32), pltpu.VMEM(sr.shape, f32)] + [dma((n,))] * 4,
        compiler_params=pltpu.CompilerParams(collective_id=2, has_side_effects=True),
        name="states",
    )(sr, rows)


def middle_kernel(lane_blocks, hq_ref, sr_ref, aux_ref, rows_ref, conv_ref, backl_ref, q_ref, gout_ref, gspec_ref,
                  near2, inv_near3, out_ref, back_ref, stream_ref, medium_ref, bspec_ref, fs_ref, ahead_scr, behind_scr):
    step = pl.program_id(0)
    width = q_ref.shape[1]
    r = sublanes()
    for part in range(width // LANES):
        lanes = slice(part * LANES, (part + 1) * LANES)
        eighths, ahead, behind = [], [], []
        for m in range(MODES):
            piece, row = place(m, step, part, lane_blocks)
            take = lambda ref, at: ref[piece, pl.ds(at + row, 1)]
            res, rate, chunk = take(rows_ref, 0), take(rows_ref, 2), take(rows_ref, 4)
            state, future = take(hq_ref, 0), take(hq_ref, 2)
            weight = res * jnp.sqrt(rate)
            single = jnp.exp(-rate)
            near = take(sr_ref, 2)
            fs_ref[piece, pl.ds(row, 1)] = take(aux_ref, 4) + single * near * state
            fs_ref[piece, pl.ds(2 + row, 1)] = take(aux_ref, 6) + single * (
                (near + take(aux_ref, 2)) * state + take(aux_ref, 0) * future + float(TOK) * chunk * state * future)
            eighths.append(jnp.broadcast_to(jnp.exp(-8.0 * rate), (8, LANES)))
            ahead.append(weight * state * powers(rate, r + 1.0))
            behind.append(weight * future * powers(rate, 8.0 - r))
        for block in range(16):
            other = 15 - block
            ahead_sum, behind_sum = ahead[0], behind[0]
            for m in range(1, MODES):
                ahead_sum = ahead_sum + ahead[m]
                behind_sum = behind_sum + behind[m]
            ahead_scr[8 * block:8 * block + 8, lanes] = ahead_sum
            behind_scr[8 * other:8 * other + 8, lanes] = behind_sum
            ahead = [value * eighth for value, eighth in zip(ahead, eighths)]
            behind = [value * eighth for value, eighth in zip(behind, eighths)]
    conv = (conv_ref[...] + ahead_scr[...]).astype(bf16).astype(f32)
    back = (backl_ref[...] + behind_scr[...]).astype(bf16)
    out_ref[...] = (q_ref[...] * conv).astype(bf16)
    stream_ref[...] = (gout_ref[...].astype(f32) * conv).astype(bf16)
    back_ref[...] = back
    bspec = dot2(near2[...], back)
    bspec_ref[...] = bspec
    sign = (1 - 2 * (lax.broadcasted_iota(jnp.int32, (TOK, width), 0) % 2)).astype(f32)
    real, imag = halves(bspec)
    late = jnp.concatenate([sign * imag, -sign * real], 0)
    medium_ref[...] = dot3(inv_near3[...], product_conj(late, gspec_ref[...])).astype(bf16)


def middle(hq, sr, aux, rows, conv, backl, query, grad_out, gspec, tables):
    channels = query.shape[1]
    width = block_width(channels)
    n = sr.shape[0]
    lanes = lambda count: split_lanes(count, width)
    mats = [tables[name] for name in ("near2", "inv_near3")]
    made = lambda count, kind: jax.ShapeDtypeStruct((count, channels), kind)
    return pl.pallas_call(
        functools.partial(middle_kernel, channels // LANES),
        grid=(channels // width,),
        out_shape=(made(TOK, bf16), made(TOK, bf16), made(TOK, bf16), made(TOK, bf16), made(256, f32), jax.ShapeDtypeStruct((n, 4, LANES), f32)),
        in_specs=[whole(n, 4, LANES), whole(n, 4, LANES), whole(n, 8, LANES), whole(n, 8, LANES), lanes(TOK), lanes(TOK), lanes(TOK), lanes(TOK), lanes(256)]
        + [whole(*mat.shape) for mat in mats],
        out_specs=[lanes(TOK)] * 4 + [lanes(256), whole(n, 4, LANES)],
        scratch_shapes=[pltpu.VMEM((TOK, width), f32)] * 2,
        name="middle",
    )(hq, sr, aux, rows, conv, backl, query, grad_out, gspec, *mats)


def tile_of(index, lane_blocks):
    rows = pl.multiple_of((index // lane_blocks) * 16, 16)
    lanes = pl.multiple_of((index % lane_blocks) * LANES, LANES)
    return (pl.ds(rows, 16), pl.ds(lanes, LANES))


def reduce_kernel(n, back_ref, medium_ref, fs_ref, next_ref, tile_ref, fsum_ref, tiles_in, fs_in, bsend, brecv, tsend, trecv, fsend, frecv):
    me = lax.axis_index("ctx")
    lane_blocks = medium_ref.shape[1] // LANES
    barrier = pltpu.get_barrier_semaphore()
    greet(barrier, n, "ctx")
    pl.semaphore_wait(barrier, n - 1)
    halo = send(back_ref, next_ref, bsend, brecv, ctx=lax.rem(me + n - 1, n))
    halo.start()

    def tile_copy(d):
        peer = lax.rem(me + d, n)
        return send(medium_ref.at[tile_of(peer, lane_blocks)], tiles_in.at[d], tsend.at[d], trecv.at[d], ctx=peer)

    def fs_copy(d):
        peer = lax.rem(me + d, n)
        return send(fs_ref.at[peer], fs_in.at[d], fsend.at[d], frecv.at[d], ctx=peer)

    def start(d):
        tile_copy(d).start()
        fs_copy(d).start()

    each(1, n, start)

    def add(d, totals):
        tile_copy(d).wait()
        fs_copy(d).wait()
        return totals[0] + tiles_in[d].astype(f32), totals[1] + fs_in[d]

    tile, sums = lax.fori_loop(1, n, add, (medium_ref[tile_of(me, lane_blocks)].astype(f32), fs_ref[me]))
    tile_ref[...] = tile.astype(bf16)
    fsum_ref[...] = sums
    halo.wait()


def reduce_medium(back, medium, fs):
    n = fs.shape[0]
    dma = pltpu.SemaphoreType.DMA
    return pl.pallas_call(
        functools.partial(reduce_kernel, n),
        out_shape=(jax.ShapeDtypeStruct(back.shape, bf16), jax.ShapeDtypeStruct((16, LANES), bf16), jax.ShapeDtypeStruct((4, LANES), f32)),
        in_specs=[VMEM_SPEC] * 3,
        out_specs=[VMEM_SPEC] * 3,
        scratch_shapes=[pltpu.VMEM((n, 16, LANES), bf16), pltpu.VMEM((n, 4, LANES), f32), dma, dma] + [dma((n,))] * 4,
        compiler_params=pltpu.CompilerParams(collective_id=3, has_side_effects=True),
        name="reduce_medium",
    )(back, medium, fs)


def backward_kernel(n, lane_blocks, inv_ref, next_ref, bspec_ref, mspec_ref, q_stream, k_ref, v_ref, normed_ref, tok_ref, prev_ref,
                    gain_ref, sf_ref, gskip_ref, far2, inv_near3, gn_ref, tail_ref, small_ref, dot_ref, pad0, pad1, pad2):
    step = pl.program_id(0)
    width = tok_ref.shape[1]
    me = lax.axis_index("ctx")
    later = jnp.where(me < n - 1, next_ref[...].astype(f32), 0.0).astype(bf16)
    spec = bspec_ref[...] + dot2(far2[...], later)
    grad_gated = dot3(inv_near3[...], product_conj(spec, mspec_ref[...]))
    streams = [
        q_stream[...].astype(f32),
        (grad_gated * v_ref[...]).astype(bf16).astype(f32),
        (grad_gated * k_ref[...]).astype(bf16).astype(f32),
    ]
    total = jnp.zeros((136, width), f32)
    rows = []
    for s, pad in enumerate((pad0, pad1, pad2)):
        pad[0:8] = jnp.zeros((8, width), f32)
        pad[8:136] = streams[s]
        pad[136:144] = jnp.zeros((8, width), f32)
        for j in range(3):
            total = total + sf_ref[3 * s + j:3 * s + j + 1] * pad[j:j + 136]
            rows.append(down(streams[s] * normed_ref[8 - j:136 - j]))
    tail = jnp.where(me >= 1, total[0:8], 0.0)
    grad_normed = total[8:136]
    gn_ref[...] = grad_normed
    tail_ref[...] = tail
    wide = tok_ref[...].astype(f32)
    inv = to_column(inv_ref[0, 0:1])
    before = to_column(inv_ref[1, 0:1])[TOK - 8:]
    rows.append(down(grad_normed * wide * inv) + down(tail * prev_ref[TOK - 16:TOK].astype(f32)[8:16] * before))
    rows.append(gskip_ref[...])
    scaled = grad_normed * gain_ref[...] * wide

    @pl.when(step == 0)
    def _():
        dot_ref[...] = jnp.zeros(dot_ref.shape, f32)
        small_ref[...] = jnp.zeros(small_ref.shape, f32)

    dots = dot_ref[...]
    for part in range(width // LANES):
        lanes = slice(part * LANES, (part + 1) * LANES)
        dots = dots + scaled[:, lanes]
        for index, row in enumerate(rows):
            piece, at = place(index, step, part, lane_blocks)
            small_ref[piece, pl.ds(at, 1)] = row[:, lanes]
    dot_ref[...] = dots


def backward(n, inv, back_next, bspec, mspec, q_stream, keys, values, normed, tokens, prev, gain, short, gskip, tables):
    channels = tokens.shape[1]
    width = block_width(channels)
    lanes = lambda count: split_lanes(count, width)
    mats = [tables[name] for name in ("far2", "inv_near3")]
    return pl.pallas_call(
        functools.partial(backward_kernel, n, channels // LANES),
        grid=(channels // width,),
        out_shape=(jax.ShapeDtypeStruct((TOK, channels), f32), jax.ShapeDtypeStruct((8, channels), f32),
                   jax.ShapeDtypeStruct((n, 2, LANES), f32), jax.ShapeDtypeStruct((TOK, LANES), f32)),
        in_specs=[whole(3, 8, TOK), lanes(TOK), lanes(256), lanes(256), lanes(TOK), lanes(TOK), lanes(TOK), lanes(136), lanes(TOK), lanes(TOK),
                  lanes(1), lanes(9), lanes(1)] + [whole(*mat.shape) for mat in mats],
        out_specs=[lanes(TOK), lanes(8), whole(n, 2, LANES), whole(TOK, LANES)],
        scratch_shapes=[pltpu.VMEM((144, width), f32)] * 3,
        name="backward",
    )(inv, back_next, bspec, mspec, q_stream, keys, values, normed, tokens, prev, gain, short, gskip, *mats)


def final_kernel(n, n_tp, total, gn_ref, tail_ref, dot_ref, small_ref, tile_ref, fsum_ref, rows_ref, tok_ref, gain_ref, inv_ref,
                 tok_out, medium_out, small_out, skip_out, res_out, decay_out,
                 medium_in, fin, fin_in, tail_in, small_in, small_sum, small_all, dots, dots_in,
                 msend, mrecv, ssend, srecv, asend, arecv, dsend, drecv, fsend, frecv, tsend, trecv):
    me = lax.axis_index("ctx")
    tp = lax.axis_index("tp")
    channels = gn_ref.shape[1]
    lane_blocks = channels // LANES
    barrier = pltpu.get_barrier_semaphore()
    greet(barrier, n, "ctx")
    greet(barrier, n_tp, "tp")
    mine = rows_ref[me]
    res, rate = mine[0:2], mine[2:4]
    first, second = fsum_ref[0:2], fsum_ref[2:4]
    root = jnp.sqrt(rate)
    fin[0:2] = root * first
    fin[2:4] = res / (n * TOK) * (first / (2.0 * root) - root * second)
    pl.semaphore_wait(barrier, n - 1 + n_tp - 1)

    tail_copy = send(tail_ref, tail_in, tsend, trecv, ctx=lax.rem(me + n - 1, n))
    tail_copy.start()

    def small_copy(d):
        peer = lax.rem(me + d, n)
        return send(small_ref.at[peer], small_in.at[d], ssend.at[d], srecv.at[d], ctx=peer)

    def medium_copy(d):
        return send(tile_ref, medium_in.at[me], msend.at[d], mrecv.at[d], ctx=lax.rem(me + d, n))

    def fin_copy(d):
        return send(fin, fin_in.at[me], fsend.at[d], frecv.at[d], ctx=lax.rem(me + d, n))

    def all_copy(d):
        return send(small_sum, small_all.at[me], asend.at[d], arecv.at[d], ctx=lax.rem(me + d, n))

    def dot_copy(d):
        return send(dots, dots_in.at[d], dsend.at[d], drecv.at[d], tp=lax.rem(tp + d, n_tp))

    each(1, n, lambda d: small_copy(d).start())

    def start(d):
        medium_copy(d).start()
        fin_copy(d).start()

    each(1, n, start)
    medium_in[me] = tile_ref[...]
    fin_in[me] = fin[...]

    tail_copy.wait()
    extra = jnp.where(me < n - 1, tail_in[...], 0.0)
    gn_last = gn_ref[TOK - 8:TOK] + extra
    tail_dot = jnp.sum(extra * gain_ref[...] * tok_ref[TOK - 16:TOK].astype(f32)[8:16], axis=1, keepdims=True)
    column = jnp.sum(dot_ref[...], axis=1, keepdims=True)
    column = jnp.concatenate([column[:TOK - 8], column[TOK - 8:] + tail_dot], 0)
    dots[...] = jnp.broadcast_to(to_row(column), dots.shape)
    for d in range(1, n_tp):
        dot_copy(d).start()

    def add(d, sums):
        small_copy(d).wait()
        return sums + small_in[d]

    small_sum[...] = lax.fori_loop(1, n, add, small_ref[me])
    each(1, n, lambda d: all_copy(d).start())
    small_all[me] = small_sum[...]

    dot_row = dots[...]
    for d in range(1, n_tp):
        dot_copy(d).wait()
        dot_row = dot_row + dots_in[d]
    inv_row = inv_ref[0]
    factor = to_column((inv_row * inv_row * inv_row * dot_row / total)[0:1])
    inv = to_column(inv_row[0:1])
    for block in range(lane_blocks):
        lanes = slice(block * LANES, (block + 1) * LANES)
        gn = jnp.concatenate([gn_ref[0:TOK - 8, lanes], gn_last[:, lanes]], 0)
        tok_out[:, lanes] = (inv * (gn * gain_ref[:, lanes]) - tok_ref[:, lanes].astype(f32) * factor).astype(bf16)

    def finish(d):
        medium_copy(d).wait()
        fin_copy(d).wait()

    each(1, n, finish)

    def spread(i):
        medium_out[tile_of(i, lane_blocks)] = medium_in[i].astype(f32)

    each(0, n, spread)
    offset = 16 * lax.rem(me, 8)
    select = (lax.broadcasted_iota(jnp.int32, (16, LANES), 0) + offset == lax.broadcasted_iota(jnp.int32, (16, LANES), 1)).astype(f32)
    home = me // 8
    pick = lambda left, right: lax.dot_general(left, right, (((1,), (1,)), ((), ())), precision=HIGHEST, preferred_element_type=f32)
    res_rows, decay_rows = [], []
    for m in range(MODES):
        row = m * lane_blocks + home
        res_rows.append(fin_in[row // 2, pl.ds(row % 2, 1)])
        decay_rows.append(fin_in[row // 2, pl.ds(2 + row % 2, 1)])
    res_out[...] = pick(select, jnp.concatenate(res_rows, 0))
    decay_out[...] = pick(select, jnp.concatenate(decay_rows, 0))
    each(1, n, lambda d: all_copy(d).wait())
    for row in range(10):
        for block in range(lane_blocks):
            index = row * lane_blocks + block
            small_out[row:row + 1, block * LANES:(block + 1) * LANES] = small_all[index // 2, pl.ds(index % 2, 1)]
    row = 10 * lane_blocks + home
    skip_row = small_all[row // 2, pl.ds(row % 2, 1)]
    skip_out[...] = pick(jnp.broadcast_to(skip_row, (8, LANES)), select)
    for d in range(1, n_tp):
        pass


def final(n, n_tp, total, gn, tail, dots, small, tile, fsum, rows, tokens, gain, inv):
    channels = tokens.shape[1]
    dma = pltpu.SemaphoreType.DMA
    return pl.pallas_call(
        functools.partial(final_kernel, n, n_tp, total),
        out_shape=(jax.ShapeDtypeStruct((TOK, channels), bf16), jax.ShapeDtypeStruct((TOK, channels), f32), jax.ShapeDtypeStruct((10, channels), f32),
                   jax.ShapeDtypeStruct((8, 16), f32), jax.ShapeDtypeStruct((16, MODES), f32), jax.ShapeDtypeStruct((16, MODES), f32)),
        in_specs=[VMEM_SPEC] * 10,
        out_specs=[VMEM_SPEC] * 6,
        scratch_shapes=[
            pltpu.VMEM((n, 16, LANES), bf16), pltpu.VMEM((4, LANES), f32), pltpu.VMEM((n, 4, LANES), f32), pltpu.VMEM((8, channels), f32),
            pltpu.VMEM((n, 2, LANES), f32), pltpu.VMEM((2, LANES), f32), pltpu.VMEM((n, 2, LANES), f32),
            pltpu.VMEM((8, TOK), f32), pltpu.VMEM((n_tp, 8, TOK), f32),
        ] + [dma((n,))] * 6 + [dma((n_tp,))] * 2 + [dma((n,))] * 2 + [dma, dma],
        compiler_params=pltpu.CompilerParams(collective_id=4, has_side_effects=True),
        name="final",
    )(gn, tail, dots, small, tile, fsum, rows, tokens, gain, inv)


def per_device(tokens, norm_gain, short_filter, medium_filter, residues, decay_rate, skip_gain, grad_out):
    channels = tokens.shape[1]
    n, n_tp = lax.axis_size("ctx"), lax.axis_size("tp")
    total = channels * n_tp
    tables = {name: jnp.asarray(table) for name, table in transform_tables().items()}
    order = jnp.asarray(lane_orders())
    gain = norm_gain.reshape(1, channels)
    short = short_filter.reshape(9, channels)
    inv, prev, prev2, par = entry(tokens, residues, decay_rate, skip_gain, total)
    query, keys, values, normed, gspec, mspec, conv, backl, gskip, sr, aux, rows = forward(
        inv, tokens, prev, prev2, gain, short, medium_filter, par, grad_out, tables, order)
    hq = states(sr, rows)
    block_out, back, q_stream, medium_part, bspec, fs = middle(hq, sr, aux, rows, conv, backl, query, grad_out, gspec, tables)
    back_next, tile, fsum = reduce_medium(back, medium_part, fs)
    gn, tail, small, dots = backward(n, inv, back_next, bspec, mspec, q_stream, keys, values, normed, tokens, prev, gain, short, gskip, tables)
    grad_tokens, grad_medium, small_out, skip_out, grad_residues, grad_decay = final(
        n, n_tp, total, gn, tail, dots, small, tile, fsum, rows, tokens, gain, inv)
    return (block_out, grad_tokens, small_out[9], small_out[:9].reshape(3, 3, channels), grad_medium, skip_out[0], grad_residues, grad_decay)


def solution(mesh):
    cols = P(("tp", "ctx"), None)
    specs = (P("ctx", "tp"), P("tp"), P(None, None, "tp"), P(None, "tp"), cols, cols, P(("tp", "ctx")), P("ctx", "tp"))
    outs = (P("ctx", "tp"), P("ctx", "tp"), P("tp"), P(None, None, "tp"), P(None, "tp"), P(("tp", "ctx")), cols, cols)
    return jax.shard_map(per_device, mesh=mesh, in_specs=specs, out_specs=outs, check_vma=False)
```

```python
import functools
import math

import jax
import jax.numpy as jnp
import ml_dtypes
import numpy as np
from jax import lax
from jax.experimental import pallas as pl
from jax.experimental.pallas import tpu as pltpu
from jax.sharding import PartitionSpec as P

EPSILON = 1e-06
HIGHEST = lax.Precision.HIGHEST
MESH = pl.DeviceIdType.MESH
TOK = 128
MODES = 16
LANES = 128
f32 = jnp.float32
bf16 = jnp.bfloat16
VMEM_SPEC = pl.BlockSpec(memory_space=pltpu.VMEM)


def transform_tables():
    freq = 2 * np.arange(TOK)[:, None] + 1
    angle = np.pi / 256.0 * ((freq * np.arange(256)[None, :]) % 512)
    table = np.concatenate([np.cos(angle), -np.sin(angle)], 0)

    def two(matrix):
        high = matrix.astype(ml_dtypes.bfloat16)
        return high, (matrix - high.astype(np.float64)).astype(ml_dtypes.bfloat16)

    high, low = two(table)
    near, far = slice(0, TOK), slice(TOK, 256)
    inv_near, inv_near_low = two(table[:, near].T / 128.0)
    inv_far, inv_far_low = two(table[:, far].T / 128.0)
    cat = lambda *parts: np.concatenate(parts, 1)
    return {
        "whole2": cat(high, low),
        "near2": cat(high[:, near], low[:, near]),
        "far2": cat(high[:, far], low[:, far]),
        "near3": cat(high[:, near], high[:, near], low[:, near]),
        "inv_near3": cat(inv_near, inv_near, inv_near_low),
        "inv_far3": cat(inv_far, inv_far, inv_far_low),
    }


def lane_orders():
    order = np.zeros((2, 64, LANES), np.float32)
    for half in range(2):
        for row in range(64):
            order[half, row, 16 * (row // 8) + 8 * half + row % 8] = 1.0
    return order


def dot2(table, data):
    return jnp.dot(table, jnp.concatenate([data, data], 0), preferred_element_type=f32)


def dot3(table, data):
    high = data.astype(bf16)
    low = (data - high.astype(f32)).astype(bf16)
    return jnp.dot(table, jnp.concatenate([high, low, high], 0), preferred_element_type=f32)


def halves(spectrum):
    return spectrum[:TOK], spectrum[TOK:]


def product(first, second):
    (a, b), (c, d) = halves(first), halves(second)
    return jnp.concatenate([a * c - b * d, a * d + b * c], 0)


def product_conj(first, second):
    (a, b), (c, d) = halves(first), halves(second)
    return jnp.concatenate([a * c + b * d, b * c - a * d], 0)


def eye(size):
    return (lax.broadcasted_iota(jnp.int32, (size, size), 0) == lax.broadcasted_iota(jnp.int32, (size, size), 1)).astype(f32)


def to_column(row):
    return jnp.sum(eye(row.shape[1]) * row, axis=1, keepdims=True)


def to_row(column):
    return jnp.sum(eye(column.shape[0]) * column, axis=0, keepdims=True)


def place(row, step, part, lane_blocks):
    if lane_blocks == 1:
        return row // 2, row % 2
    return row * (lane_blocks // 2) + step, part


def greet(barrier, count, axis):
    me = lax.axis_index(axis)

    def body(d, carry):
        pl.semaphore_signal(barrier, inc=1, device_id={axis: lax.rem(me + d, count)}, device_id_type=MESH)
        return carry

    lax.fori_loop(1, count, body, 0)


def send(src, dst, send_sem, recv_sem, **where):
    return pltpu.make_async_remote_copy(src, dst, send_sem, recv_sem, device_id=where, device_id_type=MESH)


def each(first, last, work):
    def body(d, carry):
        work(d)
        return carry

    lax.fori_loop(first, last, body, 0)


def powers(rate_row, exponents):
    return jnp.exp(-rate_row * exponents)


def sublanes():
    return lax.broadcasted_iota(jnp.int32, (8, LANES), 0).astype(f32)


def horner(blocks, eighth):
    total = blocks[-1]
    moment = jnp.zeros_like(total)
    for block in blocks[-2::-1]:
        shifted = eighth * total
        moment = eighth * moment + shifted
        total = shifted + block
    return total, moment


def down(values):
    return jnp.sum(values, axis=0, keepdims=True)


def lane_parts(width):
    return [(part, slice(part * LANES, (part + 1) * LANES)) for part in range(width // LANES)]


def eight(rate):
    return jnp.broadcast_to(jnp.exp(-8.0 * rate), (8, LANES))


def row_blocks(ref, lanes):
    return [ref[8 * b:8 * b + 8, lanes] for b in range(16)]


def signals_block(me, inv_ref, tok_ref, prev_ref, prev2_ref, gain_ref, sf_ref, mf_ref, gout_ref, whole2, near3, inv_far3,
                  q_ref, k_ref, v_ref, normed_ref, gspec_ref, mspec_ref, gskip_ref, sig, grd, ext):
    gain = gain_ref[...]

    def normed_of(values, inv_row, live):
        scale = to_column(inv_row)[TOK - values.shape[0]:]
        rounded = (values.astype(f32) * scale * gain).astype(bf16).astype(f32)
        return jnp.where(live, rounded, 0.0)

    ext[0:16] = normed_of(prev2_ref[...], inv_ref[2, 0:1], me >= 2)
    ext[16:144] = normed_of(prev_ref[...], inv_ref[1, 0:1], me >= 1)
    ext[144:272] = normed_of(tok_ref[...], inv_ref[0, 0:1], me >= 0)
    normed_ref[...] = ext[136:272]

    def stream(s, first, count):
        total = sf_ref[s, 0:1] * ext[first:first + count]
        for j in range(1, 3):
            total = total + sf_ref[s, j:j + 1] * ext[first - j:first - j + count]
        return total

    query = stream(0, 144, TOK)
    q_ref[...] = query
    keys = stream(1, 16, 256)
    values = stream(2, 16, 256)
    k_ref[...] = keys[TOK:]
    v_ref[...] = values[TOK:]
    gated = (keys * values).astype(bf16)
    gspec = dot2(whole2[...], gated)
    mspec = dot3(near3[...], mf_ref[...])
    gspec_ref[...] = gspec
    mspec_ref[...] = mspec
    sig[...] = dot3(inv_far3[...], product(gspec, mspec)).astype(bf16).astype(f32)
    grd[...] = (gout_ref[...].astype(f32) * query).astype(bf16).astype(f32)
    gskip_ref[...] = down(sig[...] * grd[...])


def sums_block(step, lane_blocks, par_ref, order_ref, sig, grd, sr_ref, aux_ref, rows_ref, skip_ref):
    r = sublanes()
    for part, lanes in lane_parts(sig.shape[1]):
        packed = par_ref[8 * part:8 * part + 8].reshape(64, LANES).T
        even = jnp.dot(packed, order_ref[0], precision=HIGHEST, preferred_element_type=f32)
        odd = jnp.dot(packed, order_ref[1], precision=HIGHEST, preferred_element_type=f32)
        res = even[0:16] + odd[16:32]
        rate = even[32:48] + odd[48:64]
        skip_ref[0:1, lanes] = even[64:65] + odd[65:66]
        chunk = jnp.exp(-float(TOK) * rate)
        for m in range(MODES):
            piece, row = place(m, step, part, lane_blocks)
            rows_ref[piece, pl.ds(row, 1)] = res[m:m + 1]
            rows_ref[piece, pl.ds(2 + row, 1)] = rate[m:m + 1]
            rows_ref[piece, pl.ds(4 + row, 1)] = chunk[m:m + 1]
            single = rate[m:m + 1]
            rising = powers(single, r)
            falling = powers(single, 7.0 - r)
            total, moment = horner(row_blocks(sig, lanes)[::-1], eight(single))
            sr_ref[piece, pl.ds(row, 1)] = down(falling * total)
            aux_ref[piece, pl.ds(row, 1)] = down(falling * (8.0 * moment + (7.0 - r) * total))
            total, moment = horner(row_blocks(grd, lanes), eight(single))
            sr_ref[piece, pl.ds(2 + row, 1)] = down(rising * total)
            aux_ref[piece, pl.ds(2 + row, 1)] = down(rising * (8.0 * moment + r * total))


def local_block(step, lane_blocks, rows_ref, skip_ref, sig, grd, near2, near3, inv_near3, conv_ref, back_ref, aux_ref, kern, kgr):
    r = sublanes()
    for part, lanes in lane_parts(sig.shape[1]):
        eighths, running = [], []
        for m in range(MODES):
            piece, row = place(m, step, part, lane_blocks)
            rate = rows_ref[piece, pl.ds(2 + row, 1)]
            eighths.append(eight(rate))
            running.append(rows_ref[piece, pl.ds(row, 1)] * jnp.sqrt(rate) * powers(rate, r))
        for block in range(16):
            total = running[0]
            for m in range(1, MODES):
                total = total + running[m]
            if block == 0:
                total = total + jnp.where(r == 0.0, skip_ref[0:1, lanes], 0.0)
            kern[8 * block:8 * block + 8, lanes] = total
            running = [value * eighth for value, eighth in zip(running, eighths)]
    kspec = dot3(near3[...], kern[...])
    uspec = dot2(near2[...], sig[...].astype(bf16))
    cspec = dot2(near2[...], grd[...].astype(bf16))
    conv_ref[...] = dot3(inv_near3[...], product(kspec, uspec))
    back_ref[...] = dot3(inv_near3[...], product_conj(cspec, kspec))
    kgr[...] = dot3(inv_near3[...], product_conj(cspec, uspec))
    for part, lanes in lane_parts(sig.shape[1]):
        for m in range(MODES):
            piece, row = place(m, step, part, lane_blocks)
            rate = rows_ref[piece, pl.ds(2 + row, 1)]
            rising = powers(rate, r)
            total, moment = horner(row_blocks(kgr, lanes), eight(rate))
            aux_ref[piece, pl.ds(4 + row, 1)] = down(rising * total)
            aux_ref[piece, pl.ds(6 + row, 1)] = down(rising * (8.0 * moment + r * total))


def back_block(step, lane_blocks, hq_ref, rows_ref, local_ref, back_ref):
    r = sublanes()
    for part, lanes in lane_parts(local_ref.shape[1]):
        eighths, behind = [], []
        for m in range(MODES):
            piece, row = place(m, step, part, lane_blocks)
            take = lambda ref, at: ref[piece, pl.ds(at + row, 1)]
            rate = take(rows_ref, 2)
            eighths.append(eight(rate))
            behind.append(take(rows_ref, 0) * jnp.sqrt(rate) * take(hq_ref, 2) * powers(rate, 8.0 - r))
        for block in range(15, -1, -1):
            total = local_ref[8 * block:8 * block + 8, lanes]
            for m in range(MODES):
                total = total + behind[m]
            local_ref[8 * block:8 * block + 8, lanes] = total
            behind = [value * eighth for value, eighth in zip(behind, eighths)]
    back_ref[...] = local_ref[...].astype(bf16)


def conv_block(step, lane_blocks, hq_ref, sr_ref, aux_ref, rows_ref, local_ref, back_ref, q_ref, gout_ref, gspec_ref,
               near2, inv_near3, out_ref, stream_ref, medium_ref, bspec_ref, fs_ref):
    r = sublanes()
    width = q_ref.shape[1]
    for part, lanes in lane_parts(width):
        eighths, ahead = [], []
        for m in range(MODES):
            piece, row = place(m, step, part, lane_blocks)
            take = lambda ref, at: ref[piece, pl.ds(at + row, 1)]
            res, rate, chunk = take(rows_ref, 0), take(rows_ref, 2), take(rows_ref, 4)
            state, future, near = take(hq_ref, 0), take(hq_ref, 2), take(sr_ref, 2)
            single = jnp.exp(-rate)
            fs_ref[piece, pl.ds(row, 1)] = take(aux_ref, 4) + single * near * state
            fs_ref[piece, pl.ds(2 + row, 1)] = take(aux_ref, 6) + single * (
                (near + take(aux_ref, 2)) * state + take(aux_ref, 0) * future + float(TOK) * chunk * state * future)
            eighths.append(eight(rate))
            ahead.append(res * jnp.sqrt(rate) * state * powers(rate, r + 1.0))
        for block in range(16):
            total = local_ref[8 * block:8 * block + 8, lanes]
            for m in range(MODES):
                total = total + ahead[m]
            local_ref[8 * block:8 * block + 8, lanes] = total
            ahead = [value * eighth for value, eighth in zip(ahead, eighths)]
    conv = local_ref[...].astype(bf16).astype(f32)
    out_ref[...] = (q_ref[...] * conv).astype(bf16)
    stream_ref[...] = (gout_ref[...].astype(f32) * conv).astype(bf16)
    bspec = dot2(near2[...], back_ref[...])
    bspec_ref[...] = bspec
    sign = (1 - 2 * (lax.broadcasted_iota(jnp.int32, (TOK, width), 0) % 2)).astype(f32)
    real, imag = halves(bspec)
    late = jnp.concatenate([sign * imag, -sign * real], 0)
    medium_ref[...] = dot3(inv_near3[...], product_conj(late, gspec_ref[...])).astype(bf16)


def backward_block(step, me, n, lane_blocks, inv_ref, next_ref, bspec_ref, mspec_ref, q_stream, k_ref, v_ref, normed_ref, tok_ref, prev_ref,
                   gain_ref, sf_ref, gskip_ref, far2, inv_near3, gn_ref, tail_ref, small_ref, dot_ref, pads):
    width = tok_ref.shape[1]
    later = jnp.where(me < n - 1, next_ref[...].astype(f32), 0.0).astype(bf16)
    spec = bspec_ref[...] + dot2(far2[...], later)
    grad_gated = dot3(inv_near3[...], product_conj(spec, mspec_ref[...]))
    streams = [
        q_stream[...].astype(f32),
        (grad_gated * v_ref[...]).astype(bf16).astype(f32),
        (grad_gated * k_ref[...]).astype(bf16).astype(f32),
    ]
    total = jnp.zeros((136, width), f32)
    rows = []
    for s in range(3):
        pad = pads.at[s]
        pad[0:8] = jnp.zeros((8, width), f32)
        pad[8:136] = streams[s]
        pad[136:144] = jnp.zeros((8, width), f32)
        for j in range(3):
            total = total + sf_ref[s, j:j + 1] * pad[j:j + 136]
            rows.append(down(streams[s] * normed_ref[8 - j:136 - j]))
    tail = jnp.where(me >= 1, total[0:8], 0.0)
    grad_normed = total[8:136]
    gn_ref[...] = grad_normed
    tail_ref[...] = tail
    wide = tok_ref[...].astype(f32)
    inv = to_column(inv_ref[0, 0:1])
    before = to_column(inv_ref[1, 0:1])[TOK - 8:]
    rows.append(down(grad_normed * wide * inv) + down(tail * prev_ref[TOK - 16:TOK].astype(f32)[8:16] * before))
    rows.append(gskip_ref[...])
    scaled = grad_normed * gain_ref[...] * wide
    dots = dot_ref[...]
    for part, lanes in lane_parts(width):
        dots = dots + scaled[:, lanes]
        for index, row in enumerate(rows):
            piece, at = place(index, step, part, lane_blocks)
            small_ref[piece, pl.ds(at, 1)] = row[:, lanes]
    dot_ref[...] = dots


def tile_of(index, lane_blocks):
    rows = pl.multiple_of((index // lane_blocks) * 16, 16)
    lanes = pl.multiple_of((index % lane_blocks) * LANES, LANES)
    return (pl.ds(rows, 16), pl.ds(lanes, LANES))


TABLES = ("whole2", "near2", "far2", "near3", "inv_near3", "inv_far3")
INPUTS = ("tok", "gout", "res", "rate", "skipg", "gain", "sf", "mf", "order") + TABLES
OUTPUTS = ("out", "gtok", "medium_all", "small_all", "fin_all")


def scratch_list(n, n_tp, channels, width):
    wide = lambda rows, kind=f32: pltpu.VMEM((rows, channels), kind)
    piece = lambda rows, kind=f32: pltpu.VMEM((n, rows, LANES), kind)
    row_tile = pltpu.VMEM((8, TOK), f32)
    dma = lambda *shape: pltpu.SemaphoreType.DMA(shape)
    entries = dict(
        inv=pltpu.VMEM((3, 8, TOK), f32), prev=wide(TOK, bf16), prev2=wide(16, bf16), par=piece(8),
        msg=pltpu.VMEM((8, LANES), f32), sums=row_tile, sums_in=pltpu.VMEM((n_tp, 8, TOK), f32), inv_own=row_tile,
        q=wide(TOK), k=wide(TOK), v=wide(TOK), normed=wide(136), gspec=wide(256), mspec=wide(256), bspec=wide(256),
        sig=wide(TOK), grd=wide(TOK), conv=wide(TOK), backl=wide(TOK), gskip=wide(1), skip=wide(1),
        sr=piece(4), aux=piece(8), rows=piece(8), inbox=piece(4), outbox=piece(4), hq=piece(4),
        back=wide(TOK, bf16), next=wide(TOK, bf16), qs=wide(TOK, bf16), medium=wide(TOK, bf16),
        fs=piece(4), tiles_in=piece(16, bf16), fs_in=piece(4), tile_red=pltpu.VMEM((16, LANES), bf16), fin=pltpu.VMEM((4, LANES), f32),
        gn=wide(TOK), tail=wide(8), tail_in=wide(8), small=piece(2), small_in=piece(2), small_sum=pltpu.VMEM((2, LANES), f32),
        dotacc=pltpu.VMEM((TOK, LANES), f32), dots=row_tile, dots_in=pltpu.VMEM((n_tp, 8, TOK), f32),
        ext=pltpu.VMEM((272, width), f32), kern=pltpu.VMEM((TOK, width), f32), kgr=pltpu.VMEM((TOK, width), f32), pads=pltpu.VMEM((3, 144, width), f32),
        par_s=dma(n), par_r=dma(n), sr_s=dma(n), sr_r=dma(n), hq_s=dma(n), hq_r=dma(n), tile_s=dma(n), tile_r=dma(n), fs_s=dma(n), fs_r=dma(n),
        small_s=dma(n), small_r=dma(n), med_s=dma(n), med_r=dma(n), all_s=dma(n), all_r=dma(n), fin_s=dma(n), fin_r=dma(n),
        sum_s=dma(n_tp), sum_r=dma(n_tp), dot_s=dma(n_tp), dot_r=dma(n_tp), near_s=dma(6), near_r=dma(6),
    )
    return entries


def main_kernel(n, n_tp, total, names, *refs):
    g = dict(zip(names, refs))
    me = lax.axis_index("ctx")
    tp = lax.axis_index("tp")
    channels = g["tok"].shape[1]
    width = block_width(channels)
    lane_blocks = channels // LANES
    steps = channels // width

    def blocks(work):
        def body(step, carry):
            start = pl.multiple_of(step * width, width)
            work(step, lambda name: g[name].at[:, pl.ds(start, width)])
            return carry

        lax.fori_loop(0, steps, body, 0)

    def peer(d):
        return lax.rem(me + d, n)

    def tp_peer(d):
        return lax.rem(tp + d, n_tp)

    def copies(source, target, name):
        return lambda d: send(source(d), target(d), g[name + "_s"].at[d], g[name + "_r"].at[d], ctx=peer(d))

    def near(index, source, target, where):
        return send(source, target, g["near_s"].at[index], g["near_r"].at[index], ctx=where)

    barrier = pltpu.get_barrier_semaphore()
    greet(barrier, n, "ctx")
    greet(barrier, n_tp, "tp")
    length = n * TOK
    msg = g["msg"]
    msg[...] = jnp.zeros(msg.shape, f32)
    msg[:, 0:16] = g["res"][0:8, :]
    msg[:, 16:32] = g["res"][8:16, :]
    msg[:, 32:48] = g["rate"][0:8, :] / length
    msg[:, 48:64] = g["rate"][8:16, :] / length
    skip_col = to_column(g["skipg"][...])
    msg[:, 64:65] = skip_col[0:8]
    msg[:, 65:66] = skip_col[8:16]
    wide = g["tok"][...].astype(f32)
    sums = g["sums"]
    sums[...] = jnp.broadcast_to(to_row(jnp.sum(wide * wide, axis=1, keepdims=True)), sums.shape)
    g["small"][...] = jnp.zeros(g["small"].shape, f32)
    g["dotacc"][...] = jnp.zeros(g["dotacc"].shape, f32)
    pl.semaphore_wait(barrier, n - 1 + n_tp - 1)

    sum_copy = lambda d: send(sums, g["sums_in"].at[d], g["sum_s"].at[d], g["sum_r"].at[d], tp=tp_peer(d))
    par_copy = copies(lambda d: msg, lambda d: g["par"].at[me], "par")
    tok_copy = near(0, g["tok"], g["prev"], peer(1))
    tok2_copy = near(1, g["tok"].at[pl.ds(TOK - 16, 16)], g["prev2"], peer(2))
    for d in range(1, n_tp):
        sum_copy(d).start()
    tok2_copy.start()
    tok_copy.start()
    each(1, n, lambda d: par_copy(d).start())
    g["par"][me] = msg[...]
    squares = sums[...]
    for d in range(1, n_tp):
        sum_copy(d).wait_recv()
        squares = squares + g["sums_in"][d]
    inv_own = g["inv_own"]
    inv_own[...] = lax.rsqrt(squares / total + EPSILON)
    inv_copies = [near(2, inv_own, g["inv"].at[1], peer(1)), near(3, inv_own, g["inv"].at[2], peer(2))]
    for copy in inv_copies:
        copy.start()
    g["inv"][0] = inv_own[...]
    for copy in inv_copies + [tok_copy, tok2_copy]:
        copy.wait()

    blocks(lambda step, at: signals_block(
        me, g["inv"], at("tok"), at("prev"), at("prev2"), at("gain"), g["sf"].at[:, :, pl.ds(pl.multiple_of(step * width, width), width)], at("mf"), at("gout"),
        g["whole2"], g["near3"], g["inv_far3"], at("q"), at("k"), at("v"), at("normed"), at("gspec"), at("mspec"), at("gskip"), at("sig"), at("grd"), g["ext"]))

    each(1, n, lambda d: par_copy(d).wait_recv())
    blocks(lambda step, at: sums_block(
        step, lane_blocks, g["par"].at[pl.ds(step * (8 * width // LANES), 8 * width // LANES)], g["order"], at("sig"), at("grd"), g["sr"], g["aux"], g["rows"], at("skip")))
    inbox, outbox, hq = g["inbox"], g["outbox"], g["hq"]
    sr_copy = copies(lambda d: g["sr"].at[peer(d)], lambda d: inbox.at[me], "sr")
    hq_copy = copies(lambda d: outbox.at[peer(d)], lambda d: hq.at[me], "hq")
    each(1, n, lambda d: sr_copy(d).start())
    inbox[me] = g["sr"][me]
    decay = g["rows"][me][4:6]
    each(1, n, lambda d: sr_copy(d).wait_recv())

    def scan(i, carry):
        ahead, behind = carry
        j = n - 1 - i
        outbox[i, 0:2] = ahead
        outbox[j, 2:4] = behind
        return decay * ahead + inbox[i][0:2], decay * behind + inbox[j][2:4]

    zero = jnp.zeros((2, LANES), f32)
    lax.fori_loop(0, n, scan, (zero, zero))
    each(1, n, lambda d: hq_copy(d).start())
    hq[me] = outbox[me]
    blocks(lambda step, at: local_block(
        step, lane_blocks, g["rows"], at("skip"), at("sig"), at("grd"), g["near2"], g["near3"], g["inv_near3"], at("conv"), at("backl"), g["aux"], g["kern"], g["kgr"]))
    each(1, n, lambda d: hq_copy(d).wait_recv())

    blocks(lambda step, at: back_block(step, lane_blocks, hq, g["rows"], at("backl"), at("back")))
    halo = near(4, g["back"], g["next"], peer(n - 1))
    halo.start()
    blocks(lambda step, at: conv_block(
        step, lane_blocks, hq, g["sr"], g["aux"], g["rows"], at("conv"), at("back"), at("q"), at("gout"), at("gspec"),
        g["near2"], g["inv_near3"], at("out"), at("qs"), at("medium"), at("bspec"), g["fs"]))
    tile_copy = copies(lambda d: g["medium"].at[tile_of(peer(d), lane_blocks)], lambda d: g["tiles_in"].at[d], "tile")
    fs_copy = copies(lambda d: g["fs"].at[peer(d)], lambda d: g["fs_in"].at[d], "fs")

    def start_sums(d):
        tile_copy(d).start()
        fs_copy(d).start()

    each(1, n, start_sums)
    halo.wait()
    blocks(lambda step, at: backward_block(
        step, me, n, lane_blocks, g["inv"], at("next"), at("bspec"), at("mspec"), at("qs"), at("k"), at("v"), at("normed"), at("tok"), at("prev"),
        at("gain"), g["sf"].at[:, :, pl.ds(pl.multiple_of(step * width, width), width)], at("gskip"), g["far2"], g["inv_near3"],
        at("gn"), at("tail"), g["small"], g["dotacc"], g["pads"]))

    tail_copy = near(5, g["tail"], g["tail_in"], peer(n - 1))
    tail_copy.start()
    small_copy = copies(lambda d: g["small"].at[peer(d)], lambda d: g["small_in"].at[d], "small")
    each(1, n, lambda d: small_copy(d).start())

    def add_tile(d, sums_now):
        tile_copy(d).wait()
        fs_copy(d).wait()
        return sums_now[0] + g["tiles_in"][d].astype(f32), sums_now[1] + g["fs_in"][d]

    tile, both = lax.fori_loop(1, n, add_tile, (g["medium"][tile_of(me, lane_blocks)].astype(f32), g["fs"][me]))
    g["tile_red"][...] = tile.astype(bf16)
    mine = g["rows"][me]
    res, rate = mine[0:2], mine[2:4]
    first, second = both[0:2], both[2:4]
    root = jnp.sqrt(rate)
    fin = g["fin"]
    fin[0:2] = root * first
    fin[2:4] = res / length * (first / (2.0 * root) - root * second)
    medium_copy = copies(lambda d: g["tile_red"], lambda d: g["medium_all"].at[me], "med")
    each(1, n, lambda d: medium_copy(d).start())
    g["medium_all"][me] = tile.astype(bf16)
    groups = max(lane_blocks // 2, 1)
    members = n // groups

    def fin_to(t):
        where = lax.rem(me, groups) * members + t
        return where, send(fin, g["fin_all"].at[me], g["fin_s"].at[t], g["fin_r"].at[me], ctx=where)

    def fin_from(t):
        owner = me // members + groups * t
        return owner, send(fin, g["fin_all"].at[owner], g["fin_s"].at[t], g["fin_r"].at[owner], ctx=owner)

    def start_fin(t):
        where, copy = fin_to(t)

        @pl.when(where != me)
        def _():
            copy.start()

    each(0, members, start_fin)
    g["fin_all"][me] = fin[...]

    tail_copy.wait()
    extra = jnp.where(me < n - 1, g["tail_in"][...], 0.0)
    gn_last = g["gn"][TOK - 8:TOK] + extra
    tail_dot = jnp.sum(extra * g["gain"][...] * g["tok"][TOK - 16:TOK].astype(f32)[8:16], axis=1, keepdims=True)
    column = jnp.sum(g["dotacc"][...], axis=1, keepdims=True)
    column = jnp.concatenate([column[:TOK - 8], column[TOK - 8:] + tail_dot], 0)
    dots = g["dots"]
    dots[...] = jnp.broadcast_to(to_row(column), dots.shape)
    dot_copy = lambda d: send(dots, g["dots_in"].at[d], g["dot_s"].at[d], g["dot_r"].at[d], tp=tp_peer(d))
    for d in range(1, n_tp):
        dot_copy(d).start()

    def add_small(d, sums_now):
        small_copy(d).wait()
        return sums_now + g["small_in"][d]

    small_sum = lax.fori_loop(1, n, add_small, g["small"][me])
    g["small_sum"][...] = small_sum
    all_copy = copies(lambda d: g["small_sum"], lambda d: g["small_all"].at[me], "all")
    each(1, n, lambda d: all_copy(d).start())
    g["small_all"][me] = small_sum

    dot_row = dots[...]
    for d in range(1, n_tp):
        dot_copy(d).wait()
        dot_row = dot_row + g["dots_in"][d]
    inv_row = g["inv"][0]
    factor = to_column((inv_row * inv_row * inv_row * dot_row / total)[0:1])
    inv = to_column(inv_row[0:1])
    for block in range(lane_blocks):
        lanes = slice(block * LANES, (block + 1) * LANES)
        gn = jnp.concatenate([g["gn"][0:TOK - 8, lanes], gn_last[:, lanes]], 0)
        g["gtok"][:, lanes] = (inv * (gn * g["gain"][:, lanes]) - g["tok"][:, lanes].astype(f32) * factor).astype(bf16)

    def finish_fin(t):
        where, out_copy = fin_to(t)
        owner, in_copy = fin_from(t)

        @pl.when(where != me)
        def _():
            out_copy.wait_send()

        @pl.when(owner != me)
        def _():
            in_copy.wait_recv()

    def finish(d):
        par_copy(d).wait_send()
        sr_copy(d).wait_send()
        hq_copy(d).wait_send()
        medium_copy(d).wait()
        all_copy(d).wait()

    for d in range(1, n_tp):
        sum_copy(d).wait_send()
    each(0, members, finish_fin)
    each(1, n, finish)


def finish_kernel(out_in, gtok_in, medium_in, small_in, fin_in, out_ref, gtok_ref, gain_ref, short_ref, medium_ref, skip_ref, res_ref, decay_ref):
    me = lax.axis_index("ctx")
    n = medium_in.shape[0]
    lane_blocks = out_in.shape[1] // LANES
    out_ref[...] = out_in[...]
    gtok_ref[...] = gtok_in[...]
    for i in range(n):
        row, lane = (i // lane_blocks) * 16, (i % lane_blocks) * LANES
        medium_ref[row:row + 16, lane:lane + LANES] = medium_in[i].astype(f32)
    offset = 16 * lax.rem(me, 8)
    select = (lax.broadcasted_iota(jnp.int32, (16, LANES), 0) + offset == lax.broadcasted_iota(jnp.int32, (16, LANES), 1)).astype(f32)
    home = me // 8
    pick = lambda left, right: lax.dot_general(left, right, (((1,), (1,)), ((), ())), precision=HIGHEST, preferred_element_type=f32)
    res_rows, decay_rows = [], []
    for m in range(MODES):
        row = m * lane_blocks + home
        res_rows.append(fin_in[row // 2, pl.ds(row % 2, 1)])
        decay_rows.append(fin_in[row // 2, pl.ds(2 + row % 2, 1)])
    res_ref[...] = pick(select, jnp.concatenate(res_rows, 0))
    decay_ref[...] = pick(select, jnp.concatenate(decay_rows, 0))
    for row in range(10):
        for block in range(lane_blocks):
            index = row * lane_blocks + block
            value = small_in[index // 2, index % 2:index % 2 + 1]
            if row == 9:
                gain_ref[0:1, block * LANES:(block + 1) * LANES] = value
            else:
                short_ref[row // 3, row % 3:row % 3 + 1, block * LANES:(block + 1) * LANES] = value
    row = 10 * lane_blocks + home
    skip_row = small_in[row // 2, pl.ds(row % 2, 1)]
    skip_ref[...] = pick(jnp.broadcast_to(skip_row, (8, LANES)), select)[0:1]


def block_width(channels):
    return min(256, channels)


def per_device(tokens, norm_gain, short_filter, medium_filter, residues, decay_rate, skip_gain, grad_out):
    channels = tokens.shape[1]
    n, n_tp = lax.axis_size("ctx"), lax.axis_size("tp")
    width = block_width(channels)
    made = transform_tables()
    tables = [jnp.asarray(made[name]) for name in TABLES]
    scratch = scratch_list(n, n_tp, channels, width)
    names = INPUTS + OUTPUTS + tuple(scratch)
    shape = jax.ShapeDtypeStruct
    results = pl.pallas_call(
        functools.partial(main_kernel, n, n_tp, channels * n_tp, names),
        out_shape=(shape((TOK, channels), bf16), shape((TOK, channels), bf16), shape((n, 16, LANES), bf16), shape((n, 2, LANES), f32), shape((n, 4, LANES), f32)),
        in_specs=[VMEM_SPEC] * len(INPUTS),
        out_specs=[VMEM_SPEC] * len(OUTPUTS),
        scratch_shapes=list(scratch.values()),
        compiler_params=pltpu.CompilerParams(collective_id=1, has_side_effects=True),
        name="block",
    )(tokens, grad_out, residues, decay_rate, skip_gain.reshape(1, -1), norm_gain.reshape(1, channels), short_filter, medium_filter, jnp.asarray(lane_orders()), *tables)
    small = skip_gain.shape[0]
    outs = pl.pallas_call(
        finish_kernel,
        out_shape=(shape((TOK, channels), bf16), shape((TOK, channels), bf16), shape((1, channels), f32), shape((3, 3, channels), f32),
                   shape((TOK, channels), f32), shape((1, small), f32), shape((small, MODES), f32), shape((small, MODES), f32)),
        in_specs=[VMEM_SPEC] * 5,
        out_specs=[VMEM_SPEC] * 8,
        name="finish",
    )(*results)
    block_out, grad_tokens, grad_gain, grad_short, grad_medium, grad_skip, grad_residues, grad_decay = outs
    return (block_out, grad_tokens, grad_gain.reshape(channels), grad_short, grad_medium, grad_skip.reshape(small), grad_residues, grad_decay)


def solution(mesh):
    cols = P(("tp", "ctx"), None)
    specs = (P("ctx", "tp"), P("tp"), P(None, None, "tp"), P(None, "tp"), cols, cols, P(("tp", "ctx")), P("ctx", "tp"))
    outs = (P("ctx", "tp"), P("ctx", "tp"), P("tp"), P(None, None, "tp"), P(None, "tp"), P(("tp", "ctx")), cols, cols)
    return jax.shard_map(per_device, mesh=mesh, in_specs=specs, out_specs=outs, check_vma=False)
```

```python
import functools
import types

import jax
import jax.numpy as jnp
import ml_dtypes
import numpy as np
from jax import lax
from jax.experimental import pallas as pl
from jax.experimental.pallas import tpu as pltpu
from jax.sharding import PartitionSpec as P

EPSILON = 1e-06
HIGHEST = lax.Precision.HIGHEST
MESH = pl.DeviceIdType.MESH
TOK = 128
MODES = 16
NX = 4
LANES = 128
f32 = jnp.float32
bf16 = jnp.bfloat16
VMEM_SPEC = pl.BlockSpec(memory_space=pltpu.VMEM)


def transform_tables():
    freq = 2 * np.arange(TOK)[:, None] + 1
    angle = np.pi / 256.0 * ((freq * np.arange(256)[None, :]) % 512)
    table = np.concatenate([np.cos(angle), -np.sin(angle)], 0)

    def two(matrix):
        high = matrix.astype(ml_dtypes.bfloat16)
        return high, (matrix - high.astype(np.float64)).astype(ml_dtypes.bfloat16)

    high, low = two(table)
    near, far = slice(0, TOK), slice(TOK, 256)
    inv_near, inv_near_low = two(table[:, near].T / 128.0)
    inv_far, inv_far_low = two(table[:, far].T / 128.0)
    cat = lambda *parts: np.concatenate(parts, 1)
    return dict(
        whole2=cat(high, low),
        near2=cat(high[:, near], low[:, near]),
        far2=cat(high[:, far], low[:, far]),
        near3=cat(high[:, near], high[:, near], low[:, near]),
        inv_near3=cat(inv_near, inv_near, inv_near_low),
        inv_far3=cat(inv_far, inv_far, inv_far_low),
    )


def lane_orders():
    order = np.zeros((2, 64, LANES), np.float32)
    for half in range(2):
        for row in range(64):
            order[half, row, 16 * (row // 8) + 8 * half + row % 8] = 1.0
    return order


def dot2(table, data):
    return jnp.dot(table, jnp.concatenate([data, data], 0), preferred_element_type=f32)


def dot3(table, data):
    high = data.astype(bf16)
    low = (data - high.astype(f32)).astype(bf16)
    return jnp.dot(table, jnp.concatenate([high, low, high], 0), preferred_element_type=f32)


def halves(spectrum):
    return spectrum[:TOK], spectrum[TOK:]


def product(first, second):
    (a, b), (c, d) = halves(first), halves(second)
    return jnp.concatenate([a * c - b * d, a * d + b * c], 0)


def product_conj(first, second):
    (a, b), (c, d) = halves(first), halves(second)
    return jnp.concatenate([a * c + b * d, b * c - a * d], 0)


def eye(size):
    return (lax.broadcasted_iota(jnp.int32, (size, size), 0) == lax.broadcasted_iota(jnp.int32, (size, size), 1)).astype(f32)


def to_column(row):
    return jnp.sum(eye(row.shape[1]) * row, axis=1, keepdims=True)


def to_row(column):
    return jnp.sum(eye(column.shape[0]) * column, axis=0, keepdims=True)


def place(row, step, part, lane_blocks):
    if lane_blocks == 1:
        return row // 2, row % 2
    return row * (lane_blocks // 2) + step, part


def greet(barrier, count, axis):
    me = lax.axis_index(axis)

    def body(d, carry):
        pl.semaphore_signal(barrier, inc=1, device_id={axis: lax.rem(me + d, count)}, device_id_type=MESH)
        return carry

    lax.fori_loop(1, count, body, 0)


def send(src, dst, send_sem, recv_sem, **where):
    return pltpu.make_async_remote_copy(src, dst, send_sem, recv_sem, device_id=where, device_id_type=MESH)


def each(first, last, work):
    def body(d, carry):
        work(d)
        return carry

    lax.fori_loop(first, last, body, 0)


def powers(rate_row, exponents):
    return jnp.exp(-rate_row * exponents)


def sublanes():
    return lax.broadcasted_iota(jnp.int32, (8, LANES), 0).astype(f32)


def horner(blocks, eighth):
    total = blocks[-1]
    moment = jnp.zeros_like(total)
    for block in blocks[-2::-1]:
        shifted = eighth * total
        moment = eighth * moment + shifted
        total = shifted + block
    return total, moment


def down(values):
    return jnp.sum(values, axis=0, keepdims=True)


def lane_parts(width):
    return [(part, slice(part * LANES, (part + 1) * LANES)) for part in range(width // LANES)]


def eight(rate):
    return jnp.broadcast_to(jnp.exp(-8.0 * rate), (8, LANES))


def row_blocks(ref, lanes):
    return [ref[8 * b:8 * b + 8, lanes] for b in range(16)]


def signals_block(me, inv_ref, tok_ref, prev_ref, prev2_ref, gain_ref, sf_ref, gout_ref, whole2, inv_far3,
                  q_ref, k_ref, v_ref, normed_ref, gspec_ref, mspec_ref, gskip_ref, sig, grd, ext):
    gain = gain_ref[...]

    def normed_of(values, inv_row, live):
        scale = to_column(inv_row)[TOK - values.shape[0]:]
        rounded = (values.astype(f32) * scale * gain).astype(bf16).astype(f32)
        return jnp.where(live, rounded, 0.0)

    ext[0:16] = normed_of(prev2_ref[...], inv_ref[2, 0:1], me >= 2)
    ext[16:144] = normed_of(prev_ref[...], inv_ref[1, 0:1], me >= 1)
    ext[144:272] = normed_of(tok_ref[...], inv_ref[0, 0:1], me >= 0)
    normed_ref[...] = ext[136:272]

    def stream(s, first, count):
        total = sf_ref[s, 0:1] * ext[first:first + count]
        for j in range(1, 3):
            total = total + sf_ref[s, j:j + 1] * ext[first - j:first - j + count]
        return total

    query = stream(0, 144, TOK)
    q_ref[...] = query
    keys = stream(1, 16, 256)
    values = stream(2, 16, 256)
    k_ref[...] = keys[TOK:]
    v_ref[...] = values[TOK:]
    gated = (keys * values).astype(bf16)
    gspec = dot2(whole2[...], gated)
    gspec_ref[...] = gspec
    sig[...] = dot3(inv_far3[...], product(gspec, mspec_ref[...])).astype(bf16).astype(f32)
    grd[...] = (gout_ref[...].astype(f32) * query).astype(bf16).astype(f32)
    gskip_ref[...] = down(sig[...] * grd[...])


def sums_block(step, lane_blocks, par_ref, order_ref, sig, grd, sr_ref, aux_ref, rows_ref, skip_ref):
    r = sublanes()
    for part, lanes in lane_parts(sig.shape[1]):
        packed = par_ref[8 * part:8 * part + 8].reshape(64, LANES).T
        even = jnp.dot(packed, order_ref[0], precision=HIGHEST, preferred_element_type=f32)
        odd = jnp.dot(packed, order_ref[1], precision=HIGHEST, preferred_element_type=f32)
        res = even[0:16] + odd[16:32]
        rate = even[32:48] + odd[48:64]
        skip_ref[0:1, lanes] = even[64:65] + odd[65:66]
        chunk = jnp.exp(-float(TOK) * rate)
        for m in range(MODES):
            piece, row = place(m, step, part, lane_blocks)
            rows_ref[piece, pl.ds(row, 1)] = res[m:m + 1]
            rows_ref[piece, pl.ds(2 + row, 1)] = rate[m:m + 1]
            rows_ref[piece, pl.ds(4 + row, 1)] = chunk[m:m + 1]
            single = rate[m:m + 1]
            rising = powers(single, r)
            falling = powers(single, 7.0 - r)
            total, moment = horner(row_blocks(sig, lanes)[::-1], eight(single))
            sr_ref[piece, pl.ds(row, 1)] = down(falling * total)
            aux_ref[piece, pl.ds(row, 1)] = down(falling * (8.0 * moment + (7.0 - r) * total))
            total, moment = horner(row_blocks(grd, lanes), eight(single))
            sr_ref[piece, pl.ds(2 + row, 1)] = down(rising * total)
            aux_ref[piece, pl.ds(2 + row, 1)] = down(rising * (8.0 * moment + r * total))


def local_block(step, lane_blocks, rows_ref, skip_ref, sig, grd, near2, near3, inv_near3, conv_ref, back_ref, aux_ref, kern, kgr):
    r = sublanes()
    for part, lanes in lane_parts(sig.shape[1]):
        eighths, running = [], []
        for m in range(MODES):
            piece, row = place(m, step, part, lane_blocks)
            rate = rows_ref[piece, pl.ds(2 + row, 1)]
            eighths.append(eight(rate))
            running.append(rows_ref[piece, pl.ds(row, 1)] * jnp.sqrt(rate) * powers(rate, r))
        for block in range(16):
            total = running[0]
            for m in range(1, MODES):
                total = total + running[m]
            if block == 0:
                total = total + jnp.where(r == 0.0, skip_ref[0:1, lanes], 0.0)
            kern[8 * block:8 * block + 8, lanes] = total
            running = [value * eighth for value, eighth in zip(running, eighths)]
    kspec = dot3(near3[...], kern[...])
    uspec = dot2(near2[...], sig[...].astype(bf16))
    cspec = dot2(near2[...], grd[...].astype(bf16))
    conv_ref[...] = dot3(inv_near3[...], product(kspec, uspec))
    back_ref[...] = dot3(inv_near3[...], product_conj(cspec, kspec))
    kgr[...] = dot3(inv_near3[...], product_conj(cspec, uspec))
    for part, lanes in lane_parts(sig.shape[1]):
        for m in range(MODES):
            piece, row = place(m, step, part, lane_blocks)
            rate = rows_ref[piece, pl.ds(2 + row, 1)]
            rising = powers(rate, r)
            total, moment = horner(row_blocks(kgr, lanes), eight(rate))
            aux_ref[piece, pl.ds(4 + row, 1)] = down(rising * total)
            aux_ref[piece, pl.ds(6 + row, 1)] = down(rising * (8.0 * moment + r * total))


def back_block(step, lane_blocks, hq_ref, rows_ref, local_ref, back_ref):
    r = sublanes()
    for part, lanes in lane_parts(local_ref.shape[1]):
        eighths, behind = [], []
        for m in range(MODES):
            piece, row = place(m, step, part, lane_blocks)
            take = lambda ref, at: ref[piece, pl.ds(at + row, 1)]
            rate = take(rows_ref, 2)
            eighths.append(eight(rate))
            behind.append(take(rows_ref, 0) * jnp.sqrt(rate) * take(hq_ref, 2) * powers(rate, 8.0 - r))
        for block in range(15, -1, -1):
            total = local_ref[8 * block:8 * block + 8, lanes]
            for m in range(MODES):
                total = total + behind[m]
            local_ref[8 * block:8 * block + 8, lanes] = total
            behind = [value * eighth for value, eighth in zip(behind, eighths)]
    back_ref[...] = local_ref[...].astype(bf16)


def medium_block(back_ref, gspec_ref, near2, inv_near3, medium_ref, bspec_ref):
    bspec = dot2(near2[...], back_ref[...])
    bspec_ref[...] = bspec
    sign = (1 - 2 * (lax.broadcasted_iota(jnp.int32, (TOK, back_ref.shape[1]), 0) % 2)).astype(f32)
    real, imag = halves(bspec)
    late = jnp.concatenate([sign * imag, -sign * real], 0)
    medium_ref[...] = dot3(inv_near3[...], product_conj(late, gspec_ref[...])).astype(bf16)


def conv_block(step, lane_blocks, hq_ref, sr_ref, aux_ref, rows_ref, local_ref, q_ref, gout_ref, out_ref, stream_ref, fs_ref):
    r = sublanes()
    width = q_ref.shape[1]
    for part, lanes in lane_parts(width):
        eighths, ahead = [], []
        for m in range(MODES):
            piece, row = place(m, step, part, lane_blocks)
            take = lambda ref, at: ref[piece, pl.ds(at + row, 1)]
            res, rate, chunk = take(rows_ref, 0), take(rows_ref, 2), take(rows_ref, 4)
            state, future, near = take(hq_ref, 0), take(hq_ref, 2), take(sr_ref, 2)
            single = jnp.exp(-rate)
            home = (step * (width // LANES) + part) * 8 + m // 2
            fs_ref[home, pl.ds(m % 2, 1)] = take(aux_ref, 4) + single * near * state
            fs_ref[home, pl.ds(2 + m % 2, 1)] = take(aux_ref, 6) + single * (
                (near + take(aux_ref, 2)) * state + take(aux_ref, 0) * future + float(TOK) * chunk * state * future)
            eighths.append(eight(rate))
            ahead.append(res * jnp.sqrt(rate) * state * powers(rate, r + 1.0))
        for block in range(16):
            total = local_ref[8 * block:8 * block + 8, lanes]
            for m in range(MODES):
                total = total + ahead[m]
            local_ref[8 * block:8 * block + 8, lanes] = total
            ahead = [value * eighth for value, eighth in zip(ahead, eighths)]
    conv = local_ref[...].astype(bf16).astype(f32)
    out_ref[...] = (q_ref[...] * conv).astype(bf16)
    stream_ref[...] = (gout_ref[...].astype(f32) * conv).astype(bf16)


def backward_block(me, n, inv_ref, next_ref, bspec_ref, mspec_ref, q_stream, k_ref, v_ref, normed_ref, tok_ref, prev_ref,
                   gain_ref, sf_ref, gskip_ref, far2, inv_near3, gn_ref, tail_ref, small_ref, dot_ref, pads):
    width = tok_ref.shape[1]
    later = jnp.where(me < n - 1, next_ref[...].astype(f32), 0.0).astype(bf16)
    spec = bspec_ref[...] + dot2(far2[...], later)
    grad_gated = dot3(inv_near3[...], product_conj(spec, mspec_ref[...]))
    streams = [
        q_stream[...].astype(f32),
        (grad_gated * v_ref[...]).astype(bf16).astype(f32),
        (grad_gated * k_ref[...]).astype(bf16).astype(f32),
    ]
    total = jnp.zeros((136, width), f32)
    rows = []
    for s in range(3):
        pad = pads.at[s]
        pad[0:8] = jnp.zeros((8, width), f32)
        pad[8:136] = streams[s]
        pad[136:144] = jnp.zeros((8, width), f32)
        for j in range(3):
            total = total + sf_ref[s, j:j + 1] * pad[j:j + 136]
            rows.append(down(streams[s] * normed_ref[8 - j:136 - j]))
    tail = jnp.where(me >= 1, total[0:8], 0.0)
    grad_normed = total[8:136]
    gn_ref[...] = grad_normed
    tail_ref[...] = tail
    wide = tok_ref[...].astype(f32)
    inv = to_column(inv_ref[0, 0:1])
    before = to_column(inv_ref[1, 0:1])[TOK - 8:]
    rows.append(down(grad_normed * wide * inv) + down(tail * prev_ref[TOK - 16:TOK].astype(f32)[8:16] * before))
    rows.append(gskip_ref[...])
    scaled = grad_normed * gain_ref[...] * wide
    dots = dot_ref[...]
    for part, lanes in lane_parts(width):
        dots = dots + scaled[:, lanes]
    dot_ref[...] = dots
    for index, row in enumerate(rows):
        small_ref[index // 2, index % 2:index % 2 + 1] = row


def scratch_list(n, n_tp, channels, width):
    wide = lambda rows, kind=f32: pltpu.VMEM((rows, channels), kind)
    piece = lambda rows, kind=f32: pltpu.VMEM((n, rows, LANES), kind)
    row_tile = pltpu.VMEM((8, TOK), f32)
    dma = lambda *shape: pltpu.SemaphoreType.DMA(shape)
    entries = dict(
        inv=pltpu.VMEM((3, 8, TOK), f32), prev=wide(TOK, bf16), prev2=wide(16, bf16), par=piece(8),
        msg=pltpu.VMEM((8, LANES), f32), sums=row_tile, sums_in=pltpu.VMEM((n_tp, 8, TOK), f32), inv_own=row_tile,
        q=wide(TOK), k=wide(TOK), v=wide(TOK), normed=wide(136), gspec=wide(256), mspec=wide(256), bspec=wide(256),
        sig=wide(TOK), grd=wide(TOK), conv=wide(TOK), backl=wide(TOK), gskip=wide(1), skip=wide(1),
        sr=piece(4), aux=piece(8), rows=piece(8), inbox=piece(4), outbox=piece(4), hq=piece(4),
        back=wide(TOK, bf16), next=wide(TOK, bf16), qs=wide(TOK, bf16), medium=wide(TOK, bf16),
        slabs_in=pltpu.VMEM((8, TOK, LANES), bf16), slab=pltpu.VMEM((TOK, LANES), bf16), tiles_in=pltpu.VMEM((8, 16, LANES), bf16),
        tile_red=pltpu.VMEM((16, LANES), bf16), slab_all=pltpu.VMEM((TOK, LANES), bf16),
        fs=piece(4), fs_in=pltpu.VMEM((8, 8, 4, LANES), f32), fs_slab=pltpu.VMEM((8, 4, LANES), f32), fsz_in=pltpu.VMEM((8, 4, LANES), f32), fin=pltpu.VMEM((4, LANES), f32),
        small=pltpu.VMEM((8, 2, channels), f32), small_in=pltpu.VMEM((8, 8, 2, LANES), f32), small_slab=pltpu.VMEM((8, 2, LANES), f32),
        smallz_in=pltpu.VMEM((8, 8, 2, LANES), f32), small_sum=pltpu.VMEM((8, 2, LANES), f32),
        tot=pltpu.VMEM((4, 4, LANES), f32), tots=pltpu.VMEM((NX, 4, 4, LANES), f32),
        gn=wide(TOK), tail=wide(8), tail_in=wide(8),
        dotacc=pltpu.VMEM((TOK, LANES), f32), dots=row_tile, dots_in=pltpu.VMEM((n_tp, 8, TOK), f32),
        ext=pltpu.VMEM((272, width), f32), kern=pltpu.VMEM((TOK, width), f32), kgr=pltpu.VMEM((TOK, width), f32), pads=pltpu.VMEM((3, 144, width), f32),
        par_s=dma(n), par_r=dma(n), sr_s=dma(16), sr_r=dma(16), hq_s=dma(16), hq_r=dma(16), tot_s=dma(NX), tot_r=dma(NX),
        mx_s=dma(8), mx_r=dma(8), mz_s=dma(8), mz_r=dma(8), az_s=dma(8), az_r=dma(8), ax_s=dma(8), ax_r=dma(8),
        fx_s=dma(8), fx_r=dma(8), fz_s=dma(8), fz_r=dma(8), fin_s=dma(8), fin_r=dma(8),
        sx_s=dma(8), sx_r=dma(8), sz_s=dma(8), sz_r=dma(8), bx_s=dma(8), bx_r=dma(8),
        sum_s=dma(n_tp), sum_r=dma(n_tp), dot_s=dma(n_tp), dot_r=dma(n_tp), near_s=dma(6), near_r=dma(6),
    )
    return entries


def main_kernel(n, n_tp, total, names, *refs):
    g = types.SimpleNamespace(**dict(zip(names, refs)))
    me = lax.axis_index("ctx")
    tp = lax.axis_index("tp")
    channels = g.tok.shape[1]
    width = block_width(channels)
    lane_blocks = channels // LANES
    steps = channels // width

    def blocks(work, first=0, last=steps):
        def body(step, carry):
            start = pl.multiple_of(step * width, width)
            work(step, lambda ref: ref.at[:, pl.ds(start, width)])
            return carry

        lax.fori_loop(first, last, body, 0)

    def peer(d):
        return lax.rem(me + d, n)

    def tp_peer(d):
        return lax.rem(tp + d, n_tp)

    row = n // NX
    me_x, spot = me // row, lax.rem(me, row)
    me_z, core = spot // 2, lax.rem(spot, 2)
    own_slab = 2 * me_x + core

    def row_peer(d):
        return lax.rem(spot + d, row)

    def x_peer(d):
        return lax.rem(me_x + d, NX)

    def slab_peer(d):
        return lax.rem(own_slab + d, 8)

    def z_peer(d):
        return lax.rem(me_z + d, 8)

    def in_row(d):
        return me_x * row + row_peer(d)

    def in_x(d):
        return x_peer(d) * row + spot

    def in_slab(d):
        other = slab_peer(d)
        return (other // 2) * row + me_z * 2 + lax.rem(other, 2)

    def in_z(d):
        return me_x * row + z_peer(d) * 2 + core

    def copies(source, target, sems, where=peer):
        return lambda d: send(source(d), target(d), sems[0].at[d], sems[1].at[d], ctx=where(d))

    def slab_lanes(index):
        return pl.ds(pl.multiple_of(index * LANES, LANES), LANES)

    def near(index, source, target, where):
        return send(source, target, g.near_s.at[index], g.near_r.at[index], ctx=where)

    barrier = pltpu.get_barrier_semaphore()
    greet(barrier, n, "ctx")
    greet(barrier, n_tp, "tp")
    length = n * TOK
    msg = g.msg
    msg[...] = jnp.zeros(msg.shape, f32)
    msg[:, 0:16] = g.res[0:8, :]
    msg[:, 16:32] = g.res[8:16, :]
    msg[:, 32:48] = g.rate[0:8, :] / length
    msg[:, 48:64] = g.rate[8:16, :] / length
    skip_col = to_column(g.skipg[...])
    msg[:, 64:65] = skip_col[0:8]
    msg[:, 65:66] = skip_col[8:16]
    wide = g.tok[...].astype(f32)
    sums = g.sums
    sums[...] = jnp.broadcast_to(to_row(jnp.sum(wide * wide, axis=1, keepdims=True)), sums.shape)
    g.small[...] = jnp.zeros(g.small.shape, f32)
    g.dotacc[...] = jnp.zeros(g.dotacc.shape, f32)

    def filter_spectrum(step, at):
        at(g.mspec)[...] = dot3(g.near3[...], at(g.mf)[...])

    blocks(filter_spectrum)
    pl.semaphore_wait(barrier, n - 1 + n_tp - 1)

    sum_copy = lambda d: send(sums, g.sums_in.at[d], g.sum_s.at[d], g.sum_r.at[d], tp=tp_peer(d))
    par_copy = copies(lambda d: msg, lambda d: g.par.at[me], (g.par_s, g.par_r))
    tok_copy = near(0, g.tok, g.prev, peer(1))
    tok2_copy = near(1, g.tok.at[pl.ds(TOK - 16, 16)], g.prev2, peer(2))
    for d in range(1, n_tp):
        sum_copy(d).start()
    tok2_copy.start()
    tok_copy.start()
    each(1, n, lambda d: par_copy(d).start())
    g.par[me] = msg[...]
    squares = sums[...]
    for d in range(1, n_tp):
        sum_copy(d).wait_recv()
        squares = squares + g.sums_in[d]
    inv_own = g.inv_own
    inv_own[...] = lax.rsqrt(squares / total + EPSILON)
    inv_copies = [near(2, inv_own, g.inv.at[1], peer(1)), near(3, inv_own, g.inv.at[2], peer(2))]
    for copy in inv_copies:
        copy.start()
    g.inv[0] = inv_own[...]
    for copy in inv_copies + [tok_copy, tok2_copy]:
        copy.wait()

    blocks(lambda step, at: signals_block(
        me, g.inv, at(g.tok), at(g.prev), at(g.prev2), at(g.gain), g.sf.at[:, :, pl.ds(pl.multiple_of(step * width, width), width)], at(g.gout),
        g.whole2, g.inv_far3, at(g.q), at(g.k), at(g.v), at(g.normed), at(g.gspec), at(g.mspec), at(g.gskip), at(g.sig), at(g.grd), g.ext))

    each(1, n, lambda d: par_copy(d).wait_recv())
    blocks(lambda step, at: sums_block(
        step, lane_blocks, g.par.at[pl.ds(step * (8 * width // LANES), 8 * width // LANES)], g.order, at(g.sig), at(g.grd), g.sr, g.aux, g.rows, at(g.skip)))
    inbox, outbox, hq = g.inbox, g.outbox, g.hq
    four = lambda index: pl.ds(4 * index, 4)
    sr_copy = copies(lambda d: g.sr.at[four(row_peer(d))], lambda d: inbox.at[four(spot)], (g.sr_s, g.sr_r), in_row)
    hq_copy = copies(lambda d: outbox.at[four(row_peer(d))], lambda d: hq.at[four(spot)], (g.hq_s, g.hq_r), in_row)
    tot_copy = copies(lambda d: g.tot, lambda d: g.tots.at[me_x], (g.tot_s, g.tot_r), in_x)
    each(1, row, lambda d: sr_copy(d).start())
    inbox[four(spot)] = g.sr[four(spot)]
    decay = g.rows[four(spot)][:, 4:6]
    row_decay = decay * decay
    row_decay = row_decay * row_decay
    row_decay = row_decay * row_decay
    row_decay = row_decay * row_decay
    each(1, row, lambda d: sr_copy(d).wait_recv())

    def advance(i, carry):
        ahead, behind = carry
        return decay * ahead + inbox[four(i)][:, 0:2], decay * behind + inbox[four(row - 1 - i)][:, 2:4]

    zero = jnp.zeros((4, 2, LANES), f32)
    ahead_total, behind_total = lax.fori_loop(0, row, advance, (zero, zero))
    g.tot[:, 0:2] = ahead_total
    g.tot[:, 2:4] = behind_total
    for d in range(1, NX):
        tot_copy(d).start()
    for d in range(1, NX):
        tot_copy(d).wait()
    before_row, after_row = zero, zero
    for x in range(NX):
        before_row = jnp.where(x < me_x, row_decay * before_row + g.tots[x][:, 0:2], before_row)
        y = NX - 1 - x
        after_row = jnp.where(y > me_x, row_decay * after_row + g.tots[y][:, 2:4], after_row)

    def scan(i, carry):
        j = row - 1 - i
        outbox[four(i), 0:2] = carry[0]
        outbox[four(j), 2:4] = carry[1]
        return advance(i, carry)

    lax.fori_loop(0, row, scan, (before_row, after_row))
    each(1, row, lambda d: hq_copy(d).start())
    hq[four(spot)] = outbox[four(spot)]
    blocks(lambda step, at: local_block(
        step, lane_blocks, g.rows, at(g.skip), at(g.sig), at(g.grd), g.near2, g.near3, g.inv_near3, at(g.conv), at(g.backl), g.aux, g.kern, g.kgr))
    each(1, row, lambda d: hq_copy(d).wait_recv())

    blocks(lambda step, at: back_block(step, lane_blocks, hq, g.rows, at(g.backl), at(g.back)))
    halo = near(4, g.back, g.next, peer(n - 1))
    halo.start()
    blocks(lambda step, at: medium_block(at(g.back), at(g.gspec), g.near2, g.inv_near3, at(g.medium), at(g.bspec)))
    mx_copy = copies(lambda d: g.medium.at[:, slab_lanes(slab_peer(d))], lambda d: g.slabs_in.at[d], (g.mx_s, g.mx_r), in_slab)
    each(1, 8, lambda d: mx_copy(d).start())
    blocks(lambda step, at: conv_block(
        step, lane_blocks, hq, g.sr, g.aux, g.rows, at(g.conv), at(g.q), at(g.gout), at(g.out), at(g.qs), g.fs))
    fs_eight = lambda index: pl.ds(8 * index, 8)
    fx_copy = copies(lambda d: g.fs.at[fs_eight(slab_peer(d))], lambda d: g.fs_in.at[d], (g.fx_s, g.fx_r), in_slab)
    each(1, 8, lambda d: fx_copy(d).start())
    halo.wait()
    work_back = lambda step, at: backward_block(
        me, n, g.inv, at(g.next), at(g.bspec), at(g.mspec), at(g.qs), at(g.k), at(g.v), at(g.normed), at(g.tok), at(g.prev),
        at(g.gain), g.sf.at[:, :, pl.ds(pl.multiple_of(step * width, width), width)], at(g.gskip), g.far2, g.inv_near3,
        at(g.gn), at(g.tail), g.small.at[:, :, pl.ds(pl.multiple_of(step * width, width), width)], g.dotacc, g.pads)
    blocks(work_back, 0, steps // 2)

    def add_all(copy, buffer, start, last=8):
        def body(d, now):
            copy(d).wait_recv()
            return now + buffer[d].astype(f32)

        return lax.fori_loop(1, last, body, start)

    g.slab[...] = add_all(mx_copy, g.slabs_in, g.medium[:, slab_lanes(own_slab)].astype(f32)).astype(bf16)
    taps = lambda index: pl.ds(pl.multiple_of(16 * index, 16), 16)
    mz_copy = copies(lambda d: g.slab.at[taps(z_peer(d))], lambda d: g.tiles_in.at[d], (g.mz_s, g.mz_r), in_z)
    each(1, 8, lambda d: mz_copy(d).start())
    g.fs_slab[...] = add_all(fx_copy, g.fs_in, g.fs[fs_eight(own_slab)])
    fz_copy = copies(lambda d: g.fs_slab.at[z_peer(d)], lambda d: g.fsz_in.at[d], (g.fz_s, g.fz_r), in_z)
    each(1, 8, lambda d: fz_copy(d).start())
    blocks(work_back, steps // 2, steps)

    tail_copy = near(5, g.tail, g.tail_in, peer(n - 1))
    tail_copy.start()
    sx_copy = copies(lambda d: g.small.at[:, :, slab_lanes(slab_peer(d))], lambda d: g.small_in.at[d], (g.sx_s, g.sx_r), in_slab)
    each(1, 8, lambda d: sx_copy(d).start())

    tile = add_all(mz_copy, g.tiles_in, g.slab[taps(me_z)].astype(f32)).astype(bf16)
    g.tile_red[...] = tile
    az_copy = copies(lambda d: g.tile_red, lambda d: g.slab_all.at[taps(me_z)], (g.az_s, g.az_r), in_z)
    each(1, 8, lambda d: az_copy(d).start())
    g.slab_all[taps(me_z)] = tile

    tail_copy.wait()
    extra = jnp.where(me < n - 1, g.tail_in[...], 0.0)
    gn_last = g.gn[TOK - 8:TOK] + extra
    tail_dot = jnp.sum(extra * g.gain[...] * g.tok[TOK - 16:TOK].astype(f32)[8:16], axis=1, keepdims=True)
    column = jnp.sum(g.dotacc[...], axis=1, keepdims=True)
    column = jnp.concatenate([column[:TOK - 8], column[TOK - 8:] + tail_dot], 0)
    dots = g.dots
    dots[...] = jnp.broadcast_to(to_row(column), dots.shape)
    dot_copy = lambda d: send(dots, g.dots_in.at[d], g.dot_s.at[d], g.dot_r.at[d], tp=tp_peer(d))
    for d in range(1, n_tp):
        dot_copy(d).start()

    g.small_slab[...] = add_all(sx_copy, g.small_in, g.small[:, :, slab_lanes(own_slab)])
    sz_copy = copies(lambda d: g.small_slab, lambda d: g.smallz_in.at[d], (g.sz_s, g.sz_r), in_z)
    each(1, 8, lambda d: sz_copy(d).start())

    both = add_all(fz_copy, g.fsz_in, g.fs_slab[me_z])
    pair = [g.rows[(2 * me_z + i) * 4 + me_x] for i in range(2)]
    pick_core = lambda rows_now, at: jnp.where(core == 0, rows_now[at:at + 1], rows_now[at + 1:at + 2])
    res = jnp.concatenate([pick_core(rows_now, 0) for rows_now in pair], 0)
    rate = jnp.concatenate([pick_core(rows_now, 2) for rows_now in pair], 0)
    first, second = both[0:2], both[2:4]
    root = jnp.sqrt(rate)
    fin = g.fin
    fin[0:2] = root * first
    fin[2:4] = res / length * (first / (2.0 * root) - root * second)

    def fin_to(t):
        where = me_x * row + core * 8 + t
        return where, send(fin, g.fin_all.at[me_z], g.fin_s.at[t], g.fin_r.at[me_z], ctx=where)

    def fin_from(t):
        owner = me_x * row + 2 * t + me_z // 4
        return owner, send(fin, g.fin_all.at[t], g.fin_s.at[t], g.fin_r.at[t], ctx=owner)

    def start_fin(t):
        where, copy = fin_to(t)

        @pl.when(where != me)
        def _():
            copy.start()

    each(0, 8, start_fin)

    @pl.when(core == me_z // 4)
    def _():
        g.fin_all[me_z] = fin[...]

    dot_row = dots[...]
    for d in range(1, n_tp):
        dot_copy(d).wait()
        dot_row = dot_row + g.dots_in[d]
    inv_row = g.inv[0]
    factor = to_column((inv_row * inv_row * inv_row * dot_row / total)[0:1])
    inv = to_column(inv_row[0:1])
    for block in range(lane_blocks):
        lanes = slice(block * LANES, (block + 1) * LANES)
        gn = jnp.concatenate([g.gn[0:TOK - 8, lanes], gn_last[:, lanes]], 0)
        g.gtok[:, lanes] = (inv * (gn * g.gain[:, lanes]) - g.tok[:, lanes].astype(f32) * factor).astype(bf16)

    small_sum = add_all(sz_copy, g.smallz_in, g.small_slab[...])
    g.small_sum[...] = small_sum
    bx_copy = copies(lambda d: g.small_sum, lambda d: g.small_all.at[:, :, slab_lanes(own_slab)], (g.bx_s, g.bx_r), in_slab)
    each(1, 8, lambda d: bx_copy(d).start())
    g.small_all[:, :, slab_lanes(own_slab)] = small_sum
    each(1, 8, lambda d: az_copy(d).wait_recv())
    ax_copy = copies(lambda d: g.slab_all, lambda d: g.medium_all.at[:, slab_lanes(own_slab)], (g.ax_s, g.ax_r), in_slab)
    each(1, 8, lambda d: ax_copy(d).start())
    g.medium_all[:, slab_lanes(own_slab)] = g.slab_all[...]

    def finish_fin(t):
        where, out_copy = fin_to(t)
        owner, in_copy = fin_from(t)

        @pl.when(where != me)
        def _():
            out_copy.wait_send()

        @pl.when(owner != me)
        def _():
            in_copy.wait_recv()

    def finish_eight(d):
        for copy in (mx_copy, fx_copy, mz_copy, fz_copy, az_copy, sx_copy, sz_copy):
            copy(d).wait_send()
        bx_copy(d).wait()
        ax_copy(d).wait()

    def finish_row(d):
        sr_copy(d).wait_send()
        hq_copy(d).wait_send()

    for d in range(1, n_tp):
        sum_copy(d).wait_send()
    each(1, n, lambda d: par_copy(d).wait_send())
    each(1, row, finish_row)
    each(0, 8, finish_fin)
    each(1, 8, finish_eight)


def finish_kernel(out_in, gtok_in, medium_in, small_in, fin_in, out_ref, gtok_ref, gain_ref, short_ref, medium_ref, skip_ref, res_ref, decay_ref):
    me = lax.axis_index("ctx")
    out_ref[...] = out_in[...]
    gtok_ref[...] = gtok_in[...]
    medium_ref[...] = medium_in[...].astype(f32)
    offset = 16 * lax.rem(me, 8)
    select = (lax.broadcasted_iota(jnp.int32, (16, LANES), 0) + offset == lax.broadcasted_iota(jnp.int32, (16, LANES), 1)).astype(f32)
    home = pl.multiple_of((me // 8) * LANES, LANES)
    pick = lambda left, right: lax.dot_general(left, right, (((1,), (1,)), ((), ())), precision=HIGHEST, preferred_element_type=f32)
    res_ref[...] = pick(select, jnp.concatenate([fin_in[i, 0:2] for i in range(8)], 0))
    decay_ref[...] = pick(select, jnp.concatenate([fin_in[i, 2:4] for i in range(8)], 0))
    for index in range(9):
        short_ref[index // 3, index % 3:index % 3 + 1] = small_in[index // 2, index % 2:index % 2 + 1]
    gain_ref[...] = small_in[4, 1:2]
    skip_row = small_in[5, 0:1, pl.ds(home, LANES)]
    skip_ref[...] = pick(jnp.broadcast_to(skip_row, (8, LANES)), select)[0:1]


def block_width(channels):
    return min(256, channels)


def per_device(tokens, norm_gain, short_filter, medium_filter, residues, decay_rate, skip_gain, grad_out):
    channels = tokens.shape[1]
    n, n_tp = lax.axis_size("ctx"), lax.axis_size("tp")
    width = block_width(channels)
    shape = jax.ShapeDtypeStruct
    inputs = dict(
        tok=tokens, gout=grad_out, res=residues, rate=decay_rate, skipg=skip_gain.reshape(1, -1), gain=norm_gain.reshape(1, channels),
        sf=short_filter, mf=medium_filter, order=jnp.asarray(lane_orders()),
        **{name: jnp.asarray(table) for name, table in transform_tables().items()})
    outputs = dict(
        out=shape((TOK, channels), bf16), gtok=shape((TOK, channels), bf16), medium_all=shape((TOK, channels), bf16),
        small_all=shape((8, 2, channels), f32), fin_all=shape((8, 4, LANES), f32))
    scratch = scratch_list(n, n_tp, channels, width)
    results = pl.pallas_call(
        functools.partial(main_kernel, n, n_tp, channels * n_tp, [*inputs, *outputs, *scratch]),
        out_shape=tuple(outputs.values()),
        in_specs=[VMEM_SPEC] * len(inputs),
        out_specs=[VMEM_SPEC] * len(outputs),
        scratch_shapes=list(scratch.values()),
        compiler_params=pltpu.CompilerParams(collective_id=1, has_side_effects=True),
        name="block",
    )(*inputs.values())
    small = skip_gain.shape[0]
    outs = pl.pallas_call(
        finish_kernel,
        out_shape=(shape((TOK, channels), bf16), shape((TOK, channels), bf16), shape((1, channels), f32), shape((3, 3, channels), f32),
                   shape((TOK, channels), f32), shape((1, small), f32), shape((small, MODES), f32), shape((small, MODES), f32)),
        in_specs=[VMEM_SPEC] * 5,
        out_specs=[VMEM_SPEC] * 8,
        name="finish",
    )(*results)
    block_out, grad_tokens, grad_gain, grad_short, grad_medium, grad_skip, grad_residues, grad_decay = outs
    return (block_out, grad_tokens, grad_gain.reshape(channels), grad_short, grad_medium, grad_skip.reshape(small), grad_residues, grad_decay)


def solution(mesh):
    cols = P(("tp", "ctx"), None)
    specs = (P("ctx", "tp"), P("tp"), P(None, None, "tp"), P(None, "tp"), cols, cols, P(("tp", "ctx")), P("ctx", "tp"))
    outs = (P("ctx", "tp"), P("ctx", "tp"), P("tp"), P(None, None, "tp"), P(None, "tp"), P(("tp", "ctx")), cols, cols)
    return jax.shard_map(per_device, mesh=mesh, in_specs=specs, out_specs=outs, check_vma=False)
```

```python
import functools
import types

import jax
import jax.numpy as jnp
import ml_dtypes
import numpy as np
from jax import lax
from jax.experimental import pallas as pl
from jax.experimental.pallas import tpu as pltpu
from jax.sharding import PartitionSpec as P

EPSILON = 1e-06
HIGHEST = lax.Precision.HIGHEST
MESH = pl.DeviceIdType.MESH
TOK = 128
MODES = 16
NX = 4
LANES = 128
f32 = jnp.float32
bf16 = jnp.bfloat16
VMEM_SPEC = pl.BlockSpec(memory_space=pltpu.VMEM)


def transform_tables():
    freq = 2 * np.arange(TOK)[:, None] + 1
    angle = np.pi / 256.0 * ((freq * np.arange(256)[None, :]) % 512)
    table = np.concatenate([np.cos(angle), -np.sin(angle)], 0)

    def two(matrix):
        high = matrix.astype(ml_dtypes.bfloat16)
        return high, (matrix - high.astype(np.float64)).astype(ml_dtypes.bfloat16)

    high, low = two(table)
    near, far = slice(0, TOK), slice(TOK, 256)
    inv_near, inv_near_low = two(table[:, near].T / 128.0)
    inv_far, inv_far_low = two(table[:, far].T / 128.0)
    cat = lambda *parts: np.concatenate(parts, 1)
    return dict(
        whole2=cat(high, low),
        near2=cat(high[:, near], low[:, near]),
        far2=cat(high[:, far], low[:, far]),
        near3=cat(high[:, near], high[:, near], low[:, near]),
        inv_near3=cat(inv_near, inv_near, inv_near_low),
        inv_far3=cat(inv_far, inv_far, inv_far_low),
    )


def lane_orders():
    order = np.zeros((2, 64, LANES), np.float32)
    for half in range(2):
        for row in range(64):
            order[half, row, 16 * (row // 8) + 8 * half + row % 8] = 1.0
    return order


def dot2(table, data):
    return jnp.dot(table, jnp.concatenate([data, data], 0), preferred_element_type=f32)


def dot3(table, data):
    high = data.astype(bf16)
    low = (data - high.astype(f32)).astype(bf16)
    return jnp.dot(table, jnp.concatenate([high, low, high], 0), preferred_element_type=f32)


def halves(spectrum):
    return spectrum[:TOK], spectrum[TOK:]


def product(first, second):
    (a, b), (c, d) = halves(first), halves(second)
    return jnp.concatenate([a * c - b * d, a * d + b * c], 0)


def product_conj(first, second):
    (a, b), (c, d) = halves(first), halves(second)
    return jnp.concatenate([a * c + b * d, b * c - a * d], 0)


def eye(size):
    return (lax.broadcasted_iota(jnp.int32, (size, size), 0) == lax.broadcasted_iota(jnp.int32, (size, size), 1)).astype(f32)


def to_column(row):
    return jnp.sum(eye(row.shape[1]) * row, axis=1, keepdims=True)


def to_row(column):
    return jnp.sum(eye(column.shape[0]) * column, axis=0, keepdims=True)


def place(row, step, part, lane_blocks):
    if lane_blocks == 1:
        return row // 2, row % 2
    return row * (lane_blocks // 2) + step, part


def send(src, dst, send_sem, recv_sem, **where):
    return pltpu.make_async_remote_copy(src, dst, send_sem, recv_sem, device_id=where, device_id_type=MESH)


def each(first, last, work):
    def body(d, carry):
        work(d)
        return carry

    lax.fori_loop(first, last, body, 0)


def powers(rate_row, exponents):
    return jnp.exp(-rate_row * exponents)


def sublanes():
    return lax.broadcasted_iota(jnp.int32, (8, LANES), 0).astype(f32)


def horner(blocks, eighth):
    total = blocks[-1]
    moment = jnp.zeros_like(total)
    for block in blocks[-2::-1]:
        shifted = eighth * total
        moment = eighth * moment + shifted
        total = shifted + block
    return total, moment


def down(values):
    return jnp.sum(values, axis=0, keepdims=True)


def lane_parts(width):
    return [(part, slice(part * LANES, (part + 1) * LANES)) for part in range(width // LANES)]


def eight(rate):
    return jnp.broadcast_to(jnp.exp(-8.0 * rate), (8, LANES))


def row_blocks(ref, lanes):
    return [ref[8 * b:8 * b + 8, lanes] for b in range(16)]


def signals_block(me, inv_ref, tok_ref, prev_ref, prev2_ref, gain_ref, sf_ref, gout_ref, whole2, inv_far3,
                  q_ref, k_ref, v_ref, normed_ref, gspec_ref, mspec_ref, gskip_ref, sig, grd, ext):
    gain = gain_ref[...]

    def normed_of(values, inv_row, live):
        scale = to_column(inv_row)[TOK - values.shape[0]:]
        rounded = (values.astype(f32) * scale * gain).astype(bf16).astype(f32)
        return jnp.where(live, rounded, 0.0)

    ext[0:16] = normed_of(prev2_ref[...], inv_ref[2, 0:1], me >= 2)
    ext[16:144] = normed_of(prev_ref[...], inv_ref[1, 0:1], me >= 1)
    ext[144:272] = normed_of(tok_ref[...], inv_ref[0, 0:1], me >= 0)
    normed_ref[...] = ext[136:272]

    def stream(s, first, count):
        total = sf_ref[s, 0:1] * ext[first:first + count]
        for j in range(1, 3):
            total = total + sf_ref[s, j:j + 1] * ext[first - j:first - j + count]
        return total

    query = stream(0, 144, TOK)
    q_ref[...] = query
    keys = stream(1, 16, 256)
    values = stream(2, 16, 256)
    k_ref[...] = keys[TOK:]
    v_ref[...] = values[TOK:]
    gated = (keys * values).astype(bf16)
    gspec = dot2(whole2[...], gated)
    gspec_ref[...] = gspec
    sig[...] = dot3(inv_far3[...], product(gspec, mspec_ref[...])).astype(bf16).astype(f32)
    grd[...] = (gout_ref[...].astype(f32) * query).astype(bf16).astype(f32)
    gskip_ref[...] = down(sig[...] * grd[...])


def sums_block(step, lane_blocks, par_ref, order_ref, sig, grd, sr_ref, aux_ref, rows_ref, skip_ref):
    r = sublanes()
    for part, lanes in lane_parts(sig.shape[1]):
        packed = par_ref[8 * part:8 * part + 8].reshape(64, LANES).T
        even = jnp.dot(packed, order_ref[0], precision=HIGHEST, preferred_element_type=f32)
        odd = jnp.dot(packed, order_ref[1], precision=HIGHEST, preferred_element_type=f32)
        res = even[0:16] + odd[16:32]
        rate = even[32:48] + odd[48:64]
        skip_ref[0:1, lanes] = even[64:65] + odd[65:66]
        chunk = jnp.exp(-float(TOK) * rate)
        for m in range(MODES):
            piece, row = place(m, step, part, lane_blocks)
            rows_ref[piece, pl.ds(row, 1)] = res[m:m + 1]
            rows_ref[piece, pl.ds(2 + row, 1)] = rate[m:m + 1]
            rows_ref[piece, pl.ds(4 + row, 1)] = chunk[m:m + 1]
            single = rate[m:m + 1]
            rising = powers(single, r)
            falling = powers(single, 7.0 - r)
            total, moment = horner(row_blocks(sig, lanes)[::-1], eight(single))
            sr_ref[piece, pl.ds(row, 1)] = down(falling * total)
            aux_ref[piece, pl.ds(row, 1)] = down(falling * (8.0 * moment + (7.0 - r) * total))
            total, moment = horner(row_blocks(grd, lanes), eight(single))
            sr_ref[piece, pl.ds(2 + row, 1)] = down(rising * total)
            aux_ref[piece, pl.ds(2 + row, 1)] = down(rising * (8.0 * moment + r * total))


def local_block(step, lane_blocks, rows_ref, skip_ref, sig, grd, near2, near3, inv_near3, conv_ref, back_ref, aux_ref, kern, kgr):
    r = sublanes()
    for part, lanes in lane_parts(sig.shape[1]):
        eighths, running = [], []
        for m in range(MODES):
            piece, row = place(m, step, part, lane_blocks)
            rate = rows_ref[piece, pl.ds(2 + row, 1)]
            eighths.append(eight(rate))
            running.append(rows_ref[piece, pl.ds(row, 1)] * jnp.sqrt(rate) * powers(rate, r))
        for block in range(16):
            total = running[0]
            for m in range(1, MODES):
                total = total + running[m]
            if block == 0:
                total = total + jnp.where(r == 0.0, skip_ref[0:1, lanes], 0.0)
            kern[8 * block:8 * block + 8, lanes] = total
            running = [value * eighth for value, eighth in zip(running, eighths)]
    kspec = dot3(near3[...], kern[...])
    uspec = dot2(near2[...], sig[...].astype(bf16))
    cspec = dot2(near2[...], grd[...].astype(bf16))
    conv_ref[...] = dot3(inv_near3[...], product(kspec, uspec))
    back_ref[...] = dot3(inv_near3[...], product_conj(cspec, kspec))
    kgr[...] = dot3(inv_near3[...], product_conj(cspec, uspec))
    for part, lanes in lane_parts(sig.shape[1]):
        for m in range(MODES):
            piece, row = place(m, step, part, lane_blocks)
            rate = rows_ref[piece, pl.ds(2 + row, 1)]
            rising = powers(rate, r)
            total, moment = horner(row_blocks(kgr, lanes), eight(rate))
            aux_ref[piece, pl.ds(4 + row, 1)] = down(rising * total)
            aux_ref[piece, pl.ds(6 + row, 1)] = down(rising * (8.0 * moment + r * total))


def back_block(step, lane_blocks, hq_ref, rows_ref, local_ref, back_ref):
    r = sublanes()
    for part, lanes in lane_parts(local_ref.shape[1]):
        eighths, behind = [], []
        for m in range(MODES):
            piece, row = place(m, step, part, lane_blocks)
            take = lambda ref, at: ref[piece, pl.ds(at + row, 1)]
            rate = take(rows_ref, 2)
            eighths.append(eight(rate))
            behind.append(take(rows_ref, 0) * jnp.sqrt(rate) * take(hq_ref, 2) * powers(rate, 8.0 - r))
        for block in range(15, -1, -1):
            total = local_ref[8 * block:8 * block + 8, lanes]
            for m in range(MODES):
                total = total + behind[m]
            local_ref[8 * block:8 * block + 8, lanes] = total
            behind = [value * eighth for value, eighth in zip(behind, eighths)]
    back_ref[...] = local_ref[...].astype(bf16)


def medium_block(back_ref, gspec_ref, near2, inv_near3, medium_ref, bspec_ref):
    bspec = dot2(near2[...], back_ref[...])
    bspec_ref[...] = bspec
    sign = (1 - 2 * (lax.broadcasted_iota(jnp.int32, (TOK, back_ref.shape[1]), 0) % 2)).astype(f32)
    real, imag = halves(bspec)
    late = jnp.concatenate([sign * imag, -sign * real], 0)
    medium_ref[...] = dot3(inv_near3[...], product_conj(late, gspec_ref[...])).astype(bf16)


def conv_block(step, lane_blocks, hq_ref, sr_ref, aux_ref, rows_ref, local_ref, q_ref, gout_ref, out_ref, stream_ref, fs_ref):
    r = sublanes()
    width = q_ref.shape[1]
    for part, lanes in lane_parts(width):
        eighths, ahead = [], []
        for m in range(MODES):
            piece, row = place(m, step, part, lane_blocks)
            take = lambda ref, at: ref[piece, pl.ds(at + row, 1)]
            res, rate, chunk = take(rows_ref, 0), take(rows_ref, 2), take(rows_ref, 4)
            state, future, near = take(hq_ref, 0), take(hq_ref, 2), take(sr_ref, 2)
            single = jnp.exp(-rate)
            home = (step * (width // LANES) + part) * 8 + m // 2
            fs_ref[home, pl.ds(m % 2, 1)] = take(aux_ref, 4) + single * near * state
            fs_ref[home, pl.ds(2 + m % 2, 1)] = take(aux_ref, 6) + single * (
                (near + take(aux_ref, 2)) * state + take(aux_ref, 0) * future + float(TOK) * chunk * state * future)
            eighths.append(eight(rate))
            ahead.append(res * jnp.sqrt(rate) * state * powers(rate, r + 1.0))
        for block in range(16):
            total = local_ref[8 * block:8 * block + 8, lanes]
            for m in range(MODES):
                total = total + ahead[m]
            local_ref[8 * block:8 * block + 8, lanes] = total
            ahead = [value * eighth for value, eighth in zip(ahead, eighths)]
    conv = local_ref[...].astype(bf16).astype(f32)
    out_ref[...] = (q_ref[...] * conv).astype(bf16)
    stream_ref[...] = (gout_ref[...].astype(f32) * conv).astype(bf16)


def backward_block(me, n, inv_ref, next_ref, bspec_ref, mspec_ref, q_stream, k_ref, v_ref, normed_ref, tok_ref, prev_ref,
                   gain_ref, sf_ref, gskip_ref, far2, inv_near3, gn_ref, tail_ref, small_ref, dot_ref, pads):
    width = tok_ref.shape[1]
    later = jnp.where(me < n - 1, next_ref[...].astype(f32), 0.0).astype(bf16)
    spec = bspec_ref[...] + dot2(far2[...], later)
    grad_gated = dot3(inv_near3[...], product_conj(spec, mspec_ref[...]))
    streams = [
        q_stream[...].astype(f32),
        (grad_gated * v_ref[...]).astype(bf16).astype(f32),
        (grad_gated * k_ref[...]).astype(bf16).astype(f32),
    ]
    total = jnp.zeros((136, width), f32)
    rows = []
    for s in range(3):
        pad = pads.at[s]
        pad[0:8] = jnp.zeros((8, width), f32)
        pad[8:136] = streams[s]
        pad[136:144] = jnp.zeros((8, width), f32)
        for j in range(3):
            total = total + sf_ref[s, j:j + 1] * pad[j:j + 136]
            rows.append(down(streams[s] * normed_ref[8 - j:136 - j]))
    tail = jnp.where(me >= 1, total[0:8], 0.0)
    grad_normed = total[8:136]
    gn_ref[...] = grad_normed
    tail_ref[...] = tail
    wide = tok_ref[...].astype(f32)
    inv = to_column(inv_ref[0, 0:1])
    before = to_column(inv_ref[1, 0:1])[TOK - 8:]
    rows.append(down(grad_normed * wide * inv) + down(tail * prev_ref[TOK - 16:TOK].astype(f32)[8:16] * before))
    rows.append(gskip_ref[...])
    scaled = grad_normed * gain_ref[...] * wide
    dots = dot_ref[...]
    for part, lanes in lane_parts(width):
        dots = dots + scaled[:, lanes]
    dot_ref[...] = dots
    for index, row in enumerate(rows):
        small_ref[index // 2, index % 2:index % 2 + 1] = row


def scratch_list(n, n_tp, channels, width):
    wide = lambda rows, kind=f32: pltpu.VMEM((rows, channels), kind)
    piece = lambda rows, kind=f32: pltpu.VMEM((n, rows, LANES), kind)
    row_tile = pltpu.VMEM((8, TOK), f32)
    dma = lambda *shape: pltpu.SemaphoreType.DMA(shape)
    entries = dict(
        inv=pltpu.VMEM((3, 8, TOK), f32), prev=wide(TOK, bf16), prev2=wide(16, bf16), par=piece(8),
        msg=pltpu.VMEM((8, LANES), f32), sums=row_tile, sums_in=pltpu.VMEM((3, n_tp, 8, TOK), f32),
        q=wide(TOK), k=wide(TOK), v=wide(TOK), normed=wide(136), gspec=wide(256), mspec=wide(256), bspec=wide(256),
        sig=wide(TOK), grd=wide(TOK), conv=wide(TOK), backl=wide(TOK), gskip=wide(1), skip=wide(1),
        sr=piece(4), aux=piece(8), rows=piece(8), inbox=piece(4), outbox=piece(4), hq=piece(4),
        back=wide(TOK, bf16), next=wide(TOK, bf16), qs=wide(TOK, bf16), medium=wide(TOK, bf16),
        slabs_in=pltpu.VMEM((8, TOK, LANES), bf16), slab=pltpu.VMEM((TOK, LANES), bf16), tiles_in=pltpu.VMEM((8, 16, LANES), bf16),
        tile_red=pltpu.VMEM((16, LANES), bf16), slab_all=pltpu.VMEM((TOK, LANES), bf16),
        fs=piece(4), fs_in=pltpu.VMEM((8, 8, 4, LANES), f32), fs_slab=pltpu.VMEM((8, 4, LANES), f32), fsz_in=pltpu.VMEM((8, 4, LANES), f32), fin=pltpu.VMEM((4, LANES), f32),
        small=pltpu.VMEM((8, 2, channels), f32), small_in=pltpu.VMEM((8, 8, 2, LANES), f32), small_slab=pltpu.VMEM((8, 2, LANES), f32),
        smallz_in=pltpu.VMEM((8, 8, 2, LANES), f32), small_sum=pltpu.VMEM((8, 2, LANES), f32),
        tot=pltpu.VMEM((4, 4, LANES), f32), tots=pltpu.VMEM((NX, 4, 4, LANES), f32),
        gn=wide(TOK), tail=wide(8), tail_in=wide(8),
        dotacc=pltpu.VMEM((TOK, LANES), f32), dots=row_tile, dots_in=pltpu.VMEM((n_tp, 8, TOK), f32),
        ext=pltpu.VMEM((272, width), f32), kern=pltpu.VMEM((TOK, width), f32), kgr=pltpu.VMEM((TOK, width), f32), pads=pltpu.VMEM((3, 144, width), f32),
        par_s=dma(16), par_r=dma(16), parx_s=dma(NX), parx_r=dma(NX), sr_s=dma(16), sr_r=dma(16), hq_s=dma(16), hq_r=dma(16), tot_s=dma(NX), tot_r=dma(NX),
        mx_s=dma(8), mx_r=dma(8), mz_s=dma(8), mz_r=dma(8), az_s=dma(8), az_r=dma(8), ax_s=dma(8), ax_r=dma(8),
        fx_s=dma(8), fx_r=dma(8), fz_s=dma(8), fz_r=dma(8), fin_s=dma(8), fin_r=dma(8),
        sx_s=dma(8), sx_r=dma(8), sz_s=dma(8), sz_r=dma(8), bx_s=dma(8), bx_r=dma(8),
        sum_s=dma(3 * n_tp), sum_r=dma(3 * n_tp), dot_s=dma(n_tp), dot_r=dma(n_tp), near_s=dma(6), near_r=dma(6),
    )
    return entries


def main_kernel(n, n_tp, total, names, *refs):
    g = types.SimpleNamespace(**dict(zip(names, refs)))
    me = lax.axis_index("ctx")
    tp = lax.axis_index("tp")
    channels = g.tok.shape[1]
    width = block_width(channels)
    lane_blocks = channels // LANES
    steps = channels // width

    def blocks(work, first=0, last=steps):
        def body(step, carry):
            start = pl.multiple_of(step * width, width)
            work(step, lambda ref: ref.at[:, pl.ds(start, width)])
            return carry

        lax.fori_loop(first, last, body, 0)

    def peer(d):
        return lax.rem(me + d, n)

    def tp_peer(d):
        return lax.rem(tp + d, n_tp)

    row = n // NX
    me_x, spot = me // row, lax.rem(me, row)
    me_z, core = spot // 2, lax.rem(spot, 2)
    own_slab = 2 * me_x + core

    def row_peer(d):
        return lax.rem(spot + d, row)

    def x_peer(d):
        return lax.rem(me_x + d, NX)

    def slab_peer(d):
        return lax.rem(own_slab + d, 8)

    def z_peer(d):
        return lax.rem(me_z + d, 8)

    def in_row(d):
        return me_x * row + row_peer(d)

    def in_x(d):
        return x_peer(d) * row + spot

    def in_slab(d):
        other = slab_peer(d)
        return (other // 2) * row + me_z * 2 + lax.rem(other, 2)

    def in_z(d):
        return me_x * row + z_peer(d) * 2 + core

    def copies(source, target, sems, where=peer):
        return lambda d: send(source(d), target(d), sems[0].at[d], sems[1].at[d], ctx=where(d))

    def slab_lanes(index):
        return pl.ds(pl.multiple_of(index * LANES, LANES), LANES)

    def near(index, source, target, where):
        return send(source, target, g.near_s.at[index], g.near_r.at[index], ctx=where)

    barrier = pltpu.get_barrier_semaphore()

    def tell(**where):
        pl.semaphore_signal(barrier, inc=1, device_id=where, device_id_type=MESH)

    each(1, row, lambda d: tell(ctx=in_row(d)))
    each(1, 8, lambda d: tell(ctx=in_slab(d)))
    for d in range(n_tp):
        if d:
            tell(tp=tp_peer(d))
        tell(ctx=peer(n - 1), tp=tp_peer(d))
        tell(ctx=peer(n - 2), tp=tp_peer(d))
    tell(ctx=peer(1))
    expected = row - 1 + 7 + 3 * n_tp
    length = n * TOK
    msg = g.msg
    msg[...] = jnp.zeros(msg.shape, f32)
    msg[:, 0:16] = g.res[0:8, :]
    msg[:, 16:32] = g.res[8:16, :]
    msg[:, 32:48] = g.rate[0:8, :] / length
    msg[:, 48:64] = g.rate[8:16, :] / length
    skip_col = to_column(g.skipg[...])
    msg[:, 64:65] = skip_col[0:8]
    msg[:, 65:66] = skip_col[8:16]
    wide = g.tok[...].astype(f32)
    sums = g.sums
    sums[...] = jnp.broadcast_to(to_row(jnp.sum(wide * wide, axis=1, keepdims=True)), sums.shape)
    g.small[...] = jnp.zeros(g.small.shape, f32)
    g.dotacc[...] = jnp.zeros(g.dotacc.shape, f32)

    def filter_spectrum(step, at):
        at(g.mspec)[...] = dot3(g.near3[...], at(g.mf)[...])

    blocks(filter_spectrum)
    pl.semaphore_wait(barrier, expected)

    sum_pairs = [(e, d) for e in range(3) for d in range(n_tp) if e or d]

    def sum_copy(e, d):
        return send(sums, g.sums_in.at[e, d], g.sum_s.at[n_tp * e + d], g.sum_r.at[n_tp * e + d], ctx=peer(e), tp=tp_peer(d))

    par_copy = copies(lambda d: msg, lambda d: g.par.at[me], (g.par_s, g.par_r), in_row)
    own_row = pl.ds(me_x * row, row)
    parx_copy = copies(lambda d: g.par.at[own_row], lambda d: g.par.at[own_row], (g.parx_s, g.parx_r), in_x)
    tok_copy = near(0, g.tok, g.prev, peer(1))
    tok2_copy = near(1, g.tok.at[pl.ds(TOK - 16, 16)], g.prev2, peer(2))
    for e, d in sum_pairs:
        sum_copy(e, d).start()
    tok2_copy.start()
    each(1, row, lambda d: par_copy(d).start())
    tok_copy.start()
    g.par[me] = msg[...]
    for e in range(3):
        squares = sums[...] if e == 0 else jnp.zeros(sums.shape, f32)
        for d in range(n_tp):
            if e or d:
                sum_copy(e, d).wait_recv()
                squares = squares + g.sums_in[e, d]
        g.inv[e] = lax.rsqrt(squares / total + EPSILON)
    each(1, row, lambda d: par_copy(d).wait_recv())
    for d in range(1, NX):
        parx_copy(d).start()
    tok2_copy.wait()
    tok_copy.wait()

    blocks(lambda step, at: signals_block(
        me, g.inv, at(g.tok), at(g.prev), at(g.prev2), at(g.gain), g.sf.at[:, :, pl.ds(pl.multiple_of(step * width, width), width)], at(g.gout),
        g.whole2, g.inv_far3, at(g.q), at(g.k), at(g.v), at(g.normed), at(g.gspec), at(g.mspec), at(g.gskip), at(g.sig), at(g.grd), g.ext))

    for d in range(1, NX):
        parx_copy(d).wait_recv()
    blocks(lambda step, at: sums_block(
        step, lane_blocks, g.par.at[pl.ds(step * (8 * width // LANES), 8 * width // LANES)], g.order, at(g.sig), at(g.grd), g.sr, g.aux, g.rows, at(g.skip)))
    inbox, outbox, hq = g.inbox, g.outbox, g.hq
    four = lambda index: pl.ds(4 * index, 4)
    sr_copy = copies(lambda d: g.sr.at[four(row_peer(d))], lambda d: inbox.at[four(spot)], (g.sr_s, g.sr_r), in_row)
    hq_copy = copies(lambda d: outbox.at[four(row_peer(d))], lambda d: hq.at[four(spot)], (g.hq_s, g.hq_r), in_row)
    tot_copy = copies(lambda d: g.tot, lambda d: g.tots.at[me_x], (g.tot_s, g.tot_r), in_x)
    each(1, row, lambda d: sr_copy(d).start())
    inbox[four(spot)] = g.sr[four(spot)]
    decay = g.rows[four(spot)][:, 4:6]
    row_decay = decay * decay
    row_decay = row_decay * row_decay
    row_decay = row_decay * row_decay
    row_decay = row_decay * row_decay
    each(1, row, lambda d: sr_copy(d).wait_recv())

    def advance(i, carry):
        ahead, behind = carry
        return decay * ahead + inbox[four(i)][:, 0:2], decay * behind + inbox[four(row - 1 - i)][:, 2:4]

    zero = jnp.zeros((4, 2, LANES), f32)
    ahead_total, behind_total = lax.fori_loop(0, row, advance, (zero, zero))
    g.tot[:, 0:2] = ahead_total
    g.tot[:, 2:4] = behind_total
    for d in range(1, NX):
        tot_copy(d).start()
    for d in range(1, NX):
        tot_copy(d).wait()
    before_row, after_row = zero, zero
    for x in range(NX):
        before_row = jnp.where(x < me_x, row_decay * before_row + g.tots[x][:, 0:2], before_row)
        y = NX - 1 - x
        after_row = jnp.where(y > me_x, row_decay * after_row + g.tots[y][:, 2:4], after_row)

    def scan(i, carry):
        j = row - 1 - i
        outbox[four(i), 0:2] = carry[0]
        outbox[four(j), 2:4] = carry[1]
        return advance(i, carry)

    lax.fori_loop(0, row, scan, (before_row, after_row))
    each(1, row, lambda d: hq_copy(d).start())
    hq[four(spot)] = outbox[four(spot)]
    blocks(lambda step, at: local_block(
        step, lane_blocks, g.rows, at(g.skip), at(g.sig), at(g.grd), g.near2, g.near3, g.inv_near3, at(g.conv), at(g.backl), g.aux, g.kern, g.kgr))
    each(1, row, lambda d: hq_copy(d).wait_recv())

    blocks(lambda step, at: back_block(step, lane_blocks, hq, g.rows, at(g.backl), at(g.back)))
    halo = near(4, g.back, g.next, peer(n - 1))
    halo.start()
    blocks(lambda step, at: medium_block(at(g.back), at(g.gspec), g.near2, g.inv_near3, at(g.medium), at(g.bspec)))
    mx_copy = copies(lambda d: g.medium.at[:, slab_lanes(slab_peer(d))], lambda d: g.slabs_in.at[d], (g.mx_s, g.mx_r), in_slab)
    each(1, 8, lambda d: mx_copy(d).start())
    blocks(lambda step, at: conv_block(
        step, lane_blocks, hq, g.sr, g.aux, g.rows, at(g.conv), at(g.q), at(g.gout), at(g.out), at(g.qs), g.fs))
    fs_eight = lambda index: pl.ds(8 * index, 8)
    fx_copy = copies(lambda d: g.fs.at[fs_eight(slab_peer(d))], lambda d: g.fs_in.at[d], (g.fx_s, g.fx_r), in_slab)
    each(1, 8, lambda d: fx_copy(d).start())
    halo.wait()
    work_back = lambda step, at: backward_block(
        me, n, g.inv, at(g.next), at(g.bspec), at(g.mspec), at(g.qs), at(g.k), at(g.v), at(g.normed), at(g.tok), at(g.prev),
        at(g.gain), g.sf.at[:, :, pl.ds(pl.multiple_of(step * width, width), width)], at(g.gskip), g.far2, g.inv_near3,
        at(g.gn), at(g.tail), g.small.at[:, :, pl.ds(pl.multiple_of(step * width, width), width)], g.dotacc, g.pads)
    blocks(work_back, 0, steps // 2)

    def add_all(copy, buffer, start, last=8):
        def body(d, now):
            copy(d).wait_recv()
            return now + buffer[d].astype(f32)

        return lax.fori_loop(1, last, body, start)

    g.slab[...] = add_all(mx_copy, g.slabs_in, g.medium[:, slab_lanes(own_slab)].astype(f32)).astype(bf16)
    taps = lambda index: pl.ds(pl.multiple_of(16 * index, 16), 16)
    mz_copy = copies(lambda d: g.slab.at[taps(z_peer(d))], lambda d: g.tiles_in.at[d], (g.mz_s, g.mz_r), in_z)
    each(1, 8, lambda d: mz_copy(d).start())
    g.fs_slab[...] = add_all(fx_copy, g.fs_in, g.fs[fs_eight(own_slab)])
    fz_copy = copies(lambda d: g.fs_slab.at[z_peer(d)], lambda d: g.fsz_in.at[d], (g.fz_s, g.fz_r), in_z)
    each(1, 8, lambda d: fz_copy(d).start())
    blocks(work_back, steps // 2, steps)

    tail_copy = near(5, g.tail, g.tail_in, peer(n - 1))
    tail_copy.start()
    sx_copy = copies(lambda d: g.small.at[:, :, slab_lanes(slab_peer(d))], lambda d: g.small_in.at[d], (g.sx_s, g.sx_r), in_slab)
    each(1, 8, lambda d: sx_copy(d).start())

    tile = add_all(mz_copy, g.tiles_in, g.slab[taps(me_z)].astype(f32)).astype(bf16)
    g.tile_red[...] = tile
    az_copy = copies(lambda d: g.tile_red, lambda d: g.slab_all.at[taps(me_z)], (g.az_s, g.az_r), in_z)
    each(1, 8, lambda d: az_copy(d).start())
    g.slab_all[taps(me_z)] = tile

    tail_copy.wait()
    extra = jnp.where(me < n - 1, g.tail_in[...], 0.0)
    gn_last = g.gn[TOK - 8:TOK] + extra
    tail_dot = jnp.sum(extra * g.gain[...] * g.tok[TOK - 16:TOK].astype(f32)[8:16], axis=1, keepdims=True)
    column = jnp.sum(g.dotacc[...], axis=1, keepdims=True)
    column = jnp.concatenate([column[:TOK - 8], column[TOK - 8:] + tail_dot], 0)
    dots = g.dots
    dots[...] = jnp.broadcast_to(to_row(column), dots.shape)
    dot_copy = lambda d: send(dots, g.dots_in.at[d], g.dot_s.at[d], g.dot_r.at[d], tp=tp_peer(d))
    for d in range(1, n_tp):
        dot_copy(d).start()

    g.small_slab[...] = add_all(sx_copy, g.small_in, g.small[:, :, slab_lanes(own_slab)])
    sz_copy = copies(lambda d: g.small_slab, lambda d: g.smallz_in.at[d], (g.sz_s, g.sz_r), in_z)
    each(1, 8, lambda d: sz_copy(d).start())

    both = add_all(fz_copy, g.fsz_in, g.fs_slab[me_z])
    pair = [g.rows[(2 * me_z + i) * 4 + me_x] for i in range(2)]
    pick_core = lambda rows_now, at: jnp.where(core == 0, rows_now[at:at + 1], rows_now[at + 1:at + 2])
    res = jnp.concatenate([pick_core(rows_now, 0) for rows_now in pair], 0)
    rate = jnp.concatenate([pick_core(rows_now, 2) for rows_now in pair], 0)
    first, second = both[0:2], both[2:4]
    root = jnp.sqrt(rate)
    fin = g.fin
    fin[0:2] = root * first
    fin[2:4] = res / length * (first / (2.0 * root) - root * second)

    def fin_to(t):
        where = me_x * row + core * 8 + t
        return where, send(fin, g.fin_all.at[me_z], g.fin_s.at[t], g.fin_r.at[me_z], ctx=where)

    def fin_from(t):
        owner = me_x * row + 2 * t + me_z // 4
        return owner, send(fin, g.fin_all.at[t], g.fin_s.at[t], g.fin_r.at[t], ctx=owner)

    def start_fin(t):
        where, copy = fin_to(t)

        @pl.when(where != me)
        def _():
            copy.start()

    each(0, 8, start_fin)

    @pl.when(core == me_z // 4)
    def _():
        g.fin_all[me_z] = fin[...]

    dot_row = dots[...]
    for d in range(1, n_tp):
        dot_copy(d).wait()
        dot_row = dot_row + g.dots_in[d]
    inv_row = g.inv[0]
    factor = to_column((inv_row * inv_row * inv_row * dot_row / total)[0:1])
    inv = to_column(inv_row[0:1])
    for block in range(lane_blocks):
        lanes = slice(block * LANES, (block + 1) * LANES)
        gn = jnp.concatenate([g.gn[0:TOK - 8, lanes], gn_last[:, lanes]], 0)
        g.gtok[:, lanes] = (inv * (gn * g.gain[:, lanes]) - g.tok[:, lanes].astype(f32) * factor).astype(bf16)

    small_sum = add_all(sz_copy, g.smallz_in, g.small_slab[...])
    g.small_sum[...] = small_sum
    bx_copy = copies(lambda d: g.small_sum, lambda d: g.small_all.at[:, :, slab_lanes(own_slab)], (g.bx_s, g.bx_r), in_slab)
    each(1, 8, lambda d: bx_copy(d).start())
    g.small_all[:, :, slab_lanes(own_slab)] = small_sum
    each(1, 8, lambda d: az_copy(d).wait_recv())
    ax_copy = copies(lambda d: g.slab_all, lambda d: g.medium_all.at[:, slab_lanes(own_slab)], (g.ax_s, g.ax_r), in_slab)
    each(1, 8, lambda d: ax_copy(d).start())
    g.medium_all[:, slab_lanes(own_slab)] = g.slab_all[...]

    def finish_fin(t):
        where, out_copy = fin_to(t)
        owner, in_copy = fin_from(t)

        @pl.when(where != me)
        def _():
            out_copy.wait_send()

        @pl.when(owner != me)
        def _():
            in_copy.wait_recv()

    def finish_eight(d):
        for copy in (mx_copy, fx_copy, mz_copy, fz_copy, az_copy, sx_copy, sz_copy):
            copy(d).wait_send()
        bx_copy(d).wait()
        ax_copy(d).wait()

    def finish_row(d):
        par_copy(d).wait_send()
        sr_copy(d).wait_send()
        hq_copy(d).wait_send()

    for e, d in sum_pairs:
        sum_copy(e, d).wait_send()
    for d in range(1, NX):
        parx_copy(d).wait_send()
    each(1, row, finish_row)
    each(0, 8, finish_fin)
    each(1, 8, finish_eight)


def finish_kernel(out_in, gtok_in, medium_in, small_in, fin_in, out_ref, gtok_ref, gain_ref, short_ref, medium_ref, skip_ref, res_ref, decay_ref):
    me = lax.axis_index("ctx")
    out_ref[...] = out_in[...]
    gtok_ref[...] = gtok_in[...]
    medium_ref[...] = medium_in[...].astype(f32)
    offset = 16 * lax.rem(me, 8)
    select = (lax.broadcasted_iota(jnp.int32, (16, LANES), 0) + offset == lax.broadcasted_iota(jnp.int32, (16, LANES), 1)).astype(f32)
    home = pl.multiple_of((me // 8) * LANES, LANES)
    pick = lambda left, right: lax.dot_general(left, right, (((1,), (1,)), ((), ())), precision=HIGHEST, preferred_element_type=f32)
    res_ref[...] = pick(select, jnp.concatenate([fin_in[i, 0:2] for i in range(8)], 0))
    decay_ref[...] = pick(select, jnp.concatenate([fin_in[i, 2:4] for i in range(8)], 0))
    for index in range(9):
        short_ref[index // 3, index % 3:index % 3 + 1] = small_in[index // 2, index % 2:index % 2 + 1]
    gain_ref[...] = small_in[4, 1:2]
    skip_row = small_in[5, 0:1, pl.ds(home, LANES)]
    skip_ref[...] = pick(jnp.broadcast_to(skip_row, (8, LANES)), select)[0:1]


def block_width(channels):
    return min(256, channels)


def per_device(tokens, norm_gain, short_filter, medium_filter, residues, decay_rate, skip_gain, grad_out):
    channels = tokens.shape[1]
    n, n_tp = lax.axis_size("ctx"), lax.axis_size("tp")
    width = block_width(channels)
    shape = jax.ShapeDtypeStruct
    inputs = dict(
        tok=tokens, gout=grad_out, res=residues, rate=decay_rate, skipg=skip_gain.reshape(1, -1), gain=norm_gain.reshape(1, channels),
        sf=short_filter, mf=medium_filter, order=jnp.asarray(lane_orders()),
        **{name: jnp.asarray(table) for name, table in transform_tables().items()})
    outputs = dict(
        out=shape((TOK, channels), bf16), gtok=shape((TOK, channels), bf16), medium_all=shape((TOK, channels), bf16),
        small_all=shape((8, 2, channels), f32), fin_all=shape((8, 4, LANES), f32))
    scratch = scratch_list(n, n_tp, channels, width)
    results = pl.pallas_call(
        functools.partial(main_kernel, n, n_tp, channels * n_tp, [*inputs, *outputs, *scratch]),
        out_shape=tuple(outputs.values()),
        in_specs=[VMEM_SPEC] * len(inputs),
        out_specs=[VMEM_SPEC] * len(outputs),
        scratch_shapes=list(scratch.values()),
        compiler_params=pltpu.CompilerParams(collective_id=1, has_side_effects=True),
        name="block",
    )(*inputs.values())
    small = skip_gain.shape[0]
    outs = pl.pallas_call(
        finish_kernel,
        out_shape=(shape((TOK, channels), bf16), shape((TOK, channels), bf16), shape((1, channels), f32), shape((3, 3, channels), f32),
                   shape((TOK, channels), f32), shape((1, small), f32), shape((small, MODES), f32), shape((small, MODES), f32)),
        in_specs=[VMEM_SPEC] * 5,
        out_specs=[VMEM_SPEC] * 8,
        name="finish",
    )(*results)
    block_out, grad_tokens, grad_gain, grad_short, grad_medium, grad_skip, grad_residues, grad_decay = outs
    return (block_out, grad_tokens, grad_gain.reshape(channels), grad_short, grad_medium, grad_skip.reshape(small), grad_residues, grad_decay)


def solution(mesh):
    cols = P(("tp", "ctx"), None)
    specs = (P("ctx", "tp"), P("tp"), P(None, None, "tp"), P(None, "tp"), cols, cols, P(("tp", "ctx")), P("ctx", "tp"))
    outs = (P("ctx", "tp"), P("ctx", "tp"), P("tp"), P(None, None, "tp"), P(None, "tp"), P(("tp", "ctx")), cols, cols)
    return jax.shard_map(per_device, mesh=mesh, in_specs=specs, out_specs=outs, check_vma=False)
```
